256 devices in a mesh: dp: 8 (over y, x_hi), tile: 32 (over z, x_lo, core).
Axes of the slice: x: 4 (x_hi: 2, x_lo: 2; x = x_hi * 2 + x_lo), y: 4, z: 8, core: 2. Of those that a mesh axis runs over, the one named last changes fastest.
Arguments:
- features: bfloat16 [8, 4, 256, 8, 192], P('dp', None, 'tile'), may hold values from -40 to 40
- out_grad: bfloat16 [8, 4, 256, 8, 192], P('dp', None, 'tile'), may hold values from -6 to 6
- weight: bfloat16 [192, 27, 192], P('tile', None, 'dp'), may hold values from -0.078125 to 0.078125
- bias: float32 [192], replicated, may hold values from -3 to 3
- gamma: float32 [192], replicated, may hold values from 0.1 to 1.9
- beta: float32 [192], replicated, may hold values from -3 to 3
- tile_clip: int32 [8, 32], P('dp'), may hold values from 0 to 30, as said below
- tile_rows: int32 [8, 32], P('dp'), may hold values from 1 to 8, as said below
- clip_cols: int32 [8, 32], P('dp'), may hold values from 4 to 8, as said below
- clip_start: int32 [8, 32], P('dp'), may hold values from 0 to 2, as said below
Outputs:
- conv_out: bfloat16 [8, 4, 256, 8, 192], P('dp', None, 'tile')
- input_grad: bfloat16 [8, 4, 256, 8, 192], P('dp', None, 'tile')
- weight_grad: float32 [192, 27, 192], P('tile', None, 'dp')
The draws below stay inside these ranges and needn't reach their ends.
Inputs may be any that keep to these rules, and one draw needn't show every extreme that they name: `tile_clip`: in each batch clip numbers start at 0 at tile 0 and rise by 0 or 1 from one tile to the next, so a clip's tiles are consecutive; tiles 0 and 1 share a clip. `tile_rows`: 8 for every tile but the last of its clip, which may have fewer. `clip_cols`: entries past a batch's last clip are not read. `clip_start`: entries past a batch's last clip are not read.
All inputs are finite; a program needn't handle non-finite values.
Results may differ from the reference program's by a relative error of at most 0.0039.
Values may be sent and summed in bfloat16 or wider, within the bound.
A program may use at most 64 MiB of HBM per device.

```python
import jax
import jax.numpy as jnp
from jax import lax

C = 192
G = 32
F = 4
TH = 8
TW = 8
ROWS = 256
N_DP = 8
N_TILE = 32


def layout(key):
    flags = (jax.random.randint(jax.random.fold_in(key, 11), (N_DP, N_TILE), 0, 3) == 0).astype(jnp.int32)
    busiest = jax.random.randint(jax.random.fold_in(key, 13), (), 0, N_DP)
    batch_index = jnp.arange(N_DP, dtype=jnp.int32)[:, None]
    flags = jnp.where(batch_index == busiest, 1, flags).astype(jnp.int32)
    flags = flags.at[:, 0].set(1).at[:, 1].set(0)
    clips = jnp.cumsum(flags, axis=1) - 1
    last_tile = jnp.concatenate([flags[:, 1:], jnp.ones((N_DP, 1), jnp.int32)], axis=1)
    partial_rows = jax.random.randint(jax.random.fold_in(key, 12), (N_DP, N_TILE), 1, TH + 1)
    rows = jnp.where(last_tile == 1, partial_rows, TH).astype(jnp.int32)
    return (clips.astype(jnp.int32), rows)


def draw_tile_clip(key, part):
    return layout(key)[0]


def draw_tile_rows(key, part):
    return layout(key)[1]


def draw_clip_cols(key, part):
    values = jax.random.randint(jax.random.fold_in(key, 21), (N_DP, N_TILE), TW // 2, TW + 1)
    return values.at[:, 0].set(TW).at[:, 1].set(TW // 2).astype(jnp.int32)


def draw_clip_start(key, part):
    values = jax.random.randint(jax.random.fold_in(key, 31), (N_DP, N_TILE), 0, 3)
    return values.at[:, 0].set(0).at[:, 1].set(2).astype(jnp.int32)


def draw_features(key, part):
    shape = (N_DP, F, TH * N_TILE, TW, C)
    row_scale = jnp.exp(jax.random.uniform(jax.random.fold_in(key, 41), (N_DP, F, TH * N_TILE, 1, 1), minval=-1.15, maxval=1.15))
    channel_scale = jnp.exp(jax.random.uniform(jax.random.fold_in(key, 42), (C,), minval=-1.15, maxval=1.15))
    base = jnp.clip(jax.random.normal(jax.random.fold_in(key, 45), shape), -4.0, 4.0)
    return (base * row_scale * channel_scale).astype(jnp.bfloat16)


def level_of(rng, extent, shards, smallest, high):
    factor_of, own = 1.0, jax.random.fold_in(rng, 6)
    for dim, parts in shards:
        draws = jnp.exp(jax.random.uniform(jax.random.fold_in(own, dim), (parts,), jnp.float32, smallest / len(shards), high / len(shards)))
        factor_of = factor_of * jnp.repeat(draws, extent[dim] // parts).reshape([-1 if axis == dim else 1 for axis in range(len(extent))])
    return factor_of


def gaussian(rng, dims, width, limit, cuts=(), held_as=jnp.bfloat16):
    drawn = width * jax.random.normal(rng, dims, jnp.float32)
    if cuts:
        drawn = drawn * level_of(rng, dims, cuts, -0.22, 0.18)
    return jnp.clip(drawn, -limit, limit).astype(held_as)


def setup_inputs(seed: int = 0) -> dict:
    keys = jax.random.split(jax.random.key(seed), 11)
    return {
        "features": draw_features(jax.random.fold_in(keys[10], 71), 0),
        "out_grad": gaussian(keys[1], (N_DP, F, ROWS, TW, C), 1.0, 6.0, ((0, 8), (2, 32))),
        "weight": gaussian(keys[2], (C, 27, C), (27 * C) ** -0.5, 0.078125, ((0, 32), (2, 8))),
        "bias": gaussian(keys[3], (C,), 0.5, 3.0, (), jnp.float32),
        "gamma": jnp.clip(1.0 + 0.18 * jax.random.normal(keys[4], (C,), jnp.float32), 0.1, 1.9),
        "beta": gaussian(keys[5], (C,), 0.5, 3.0, (), jnp.float32),
        "tile_clip": draw_tile_clip(jax.random.fold_in(keys[10], 71), 0),
        "tile_rows": draw_tile_rows(jax.random.fold_in(keys[10], 71), 0),
        "clip_cols": draw_clip_cols(jax.random.fold_in(keys[10], 71), 0),
        "clip_start": draw_clip_start(jax.random.fold_in(keys[10], 71), 0),
    }


EPSILON = 1e-05

def with_rims(tiled, keep_above, keep_below):
    zero_row = jnp.zeros_like(tiled[:1, :, :1])
    above = jnp.concatenate([zero_row, tiled[:-1, :, -1:]], axis=0) * keep_above[:, None, None, None, None]
    below = jnp.concatenate([tiled[1:, :, :1], zero_row], axis=0) * keep_below[:, None, None, None, None]
    return jnp.concatenate([above, tiled, below], axis=2)

def reference(features, out_grad, weight, bias, gamma, beta, tile_clip, tile_rows, clip_cols, clip_start):
    group_size = C // G
    tiles = jnp.arange(N_TILE, dtype=jnp.int32)
    frame_index = jnp.arange(F, dtype=jnp.int32)[None, :, None, None]
    row_index = jnp.arange(TH, dtype=jnp.int32)[None, None, :, None]
    col_index = jnp.arange(TW, dtype=jnp.int32)[None, None, None, :]
    offsets = [(a, b, e) for a in range(3) for b in range(3) for e in range(3)]

    def tile_step(total, item):
        hidden_pad, grad_pad = item
        grad_centre = grad_pad[:F, 1:TH + 1, 1:TW + 1].reshape(-1, C)
        conv_sum = jnp.zeros((F * TH * TW, C), jnp.float32)
        hidden_grad = jnp.zeros((F * TH * TW, C), jnp.float32)
        pieces = []
        for tap, (a, b, e) in enumerate(offsets):
            hidden_slice = hidden_pad[a:a + F, b:b + TH, e:e + TW].reshape(-1, C)
            grad_slice = grad_pad[2 - a:2 - a + F, 2 - b:2 - b + TH, 2 - e:2 - e + TW].reshape(-1, C)
            tap_weight = weight[:, tap, :]
            conv_sum = conv_sum + jnp.dot(hidden_slice, tap_weight, preferred_element_type=jnp.float32)
            hidden_grad = hidden_grad + jnp.dot(grad_slice, tap_weight.T, preferred_element_type=jnp.float32)
            pieces.append(jnp.dot(hidden_slice.T, grad_centre, preferred_element_type=jnp.float32))
        return (total + jnp.stack(pieces, axis=1), (conv_sum, hidden_grad))

    def row_step(total, item):
        feats, grads_in, clips, rows, cols_table, start_table = item
        tiled = feats.reshape(F, N_TILE, TH, TW, C).transpose(1, 0, 2, 3, 4)
        grad_tiled = grads_in.reshape(F, N_TILE, TH, TW, C).transpose(1, 0, 2, 3, 4)
        cols = jnp.take(cols_table, clips)
        first = jnp.take(start_table, clips)
        valid = ((frame_index >= first[:, None, None, None]) & (row_index < rows[:, None, None, None]) & (col_index < cols[:, None, None, None])).astype(jnp.float32)[..., None]
        same = clips[:, None] == clips[None, :]
        clip_rows = lax.optimization_barrier(jnp.sum(jnp.where(same, rows[None, :], 0), axis=1))
        counted = ((F - first) * cols * clip_rows * group_size).astype(jnp.float32)[:, None]

        def clip_total(part):
            return lax.optimization_barrier(jnp.sum(jnp.where(same[:, :, None], part[None, :, :], 0.0), axis=1))
        masked = tiled.astype(jnp.float32) * valid
        grouped = masked.reshape(N_TILE, F, TH, TW, G, group_size)
        first_sum = lax.optimization_barrier(jnp.sum(grouped, axis=(1, 2, 3, 5)))
        square_sum = lax.optimization_barrier(jnp.sum(grouped * grouped, axis=(1, 2, 3, 5)))
        mean_value = clip_total(first_sum) / counted
        variance = clip_total(square_sum) / counted - mean_value * mean_value
        inv_std = lax.rsqrt(variance + EPSILON)
        expand = (slice(None), None, None, None, slice(None), None)
        normed_groups = (grouped - mean_value[expand]) * inv_std[expand]
        normed = normed_groups.reshape(N_TILE, F, TH, TW, C)
        activation = normed * gamma + beta
        sigmoid_act = jax.nn.sigmoid(activation)
        hidden = (activation * sigmoid_act * valid).astype(jnp.bfloat16)
        grad_masked = (grad_tiled.astype(jnp.float32) * valid).astype(jnp.bfloat16)
        keep_above = ((tiles > 0) & (jnp.roll(clips, 1) == clips)).astype(jnp.bfloat16)
        keep_below = ((tiles < N_TILE - 1) & (jnp.roll(clips, -1) == clips)).astype(jnp.bfloat16)
        hidden_pad = jnp.pad(with_rims(hidden, keep_above, keep_below), ((0, 0), (2, 0), (0, 0), (1, 1), (0, 0)))
        grad_pad = jnp.pad(with_rims(grad_masked, keep_above, keep_below), ((0, 0), (0, 2), (0, 0), (1, 1), (0, 0)))
        total, (conv_sum, hidden_grad) = lax.scan(tile_step, total, (hidden_pad, grad_pad))
        conv_sum = conv_sum.reshape(N_TILE, F, TH, TW, C)
        hidden_grad = hidden_grad.reshape(N_TILE, F, TH, TW, C)
        conv_out = ((conv_sum + bias) * valid).astype(jnp.bfloat16)
        dnormed = hidden_grad * valid * sigmoid_act * (1.0 + activation * (1.0 - sigmoid_act)) * gamma
        dgroups = dnormed.reshape(N_TILE, F, TH, TW, G, group_size)
        first_total = clip_total(lax.optimization_barrier(jnp.sum(dgroups, axis=(1, 2, 3, 5)))) / counted
        second_total = clip_total(lax.optimization_barrier(jnp.sum(dgroups * normed_groups, axis=(1, 2, 3, 5)))) / counted
        input_groups = inv_std[expand] * (dgroups - first_total[expand] - normed_groups * second_total[expand])
        input_grad = (input_groups.reshape(N_TILE, F, TH, TW, C) * valid).astype(jnp.bfloat16)
        conv_row = conv_out.transpose(1, 0, 2, 3, 4).reshape(F, N_TILE * TH, TW, C)
        grad_row = input_grad.transpose(1, 0, 2, 3, 4).reshape(F, N_TILE * TH, TW, C)
        return (total, (conv_row, grad_row))
    start_total = jnp.zeros((C, 27, C), jnp.float32)
    weight_grad, (conv_out, input_grad) = lax.scan(row_step, start_total, (features, out_grad, tile_clip, tile_rows, clip_cols, clip_start))
    return (conv_out, input_grad, weight_grad)
```

```python
import functools

import jax
import jax.numpy as jnp
from jax import lax
from jax.experimental import pallas as pl
from jax.experimental.pallas import tpu as pltpu
from jax.sharding import PartitionSpec as P


MESH = pl.DeviceIdType.MESH
F32, BF16, I32 = jnp.float32, jnp.bfloat16, jnp.int32
EPSILON = 1e-05
NT_DIMS = (((1,), (1,)), ((), ()))


def iota(shape, dim):
    return lax.broadcasted_iota(I32, shape, dim)


def in_channel(lane):
    group, r = (((lane >> 4) & 7) * 4 + (lane >> 7) * 2 + ((lane >> 3) & 1)), lane & 7
    return jnp.where(r < 6, group * 6 + r, -1)


def out_channel(lane):
    kind, m = lane >> 7, lane & 127
    d, j = m >> 4, m & 15
    tail = jnp.where(kind == 1, jnp.where(j < 8, d * 24 + 16 + j, -1), jnp.where(j >= 8, d * 24 + 8 + j, -1))
    return jnp.where(kind == 0, d * 24 + j, tail)


def one_hot(equal, dtype):
    return jnp.where(equal, 1.0, 0.0).astype(dtype)


def dot(a, b):
    return jnp.dot(a, b, preferred_element_type=F32)


def exact_dot(a, b):
    return jnp.dot(a, b, preferred_element_type=F32, precision=lax.Precision.HIGHEST)


def twice(mask):
    return jnp.concatenate([mask, mask], axis=1)


def group_sum(s):
    lane = iota(s.shape, 1)
    for shift in (1, 2, 4):
        s = s + jnp.where((lane & shift) != 0, pltpu.roll(s, shift, 1), pltpu.roll(s, 128 - shift, 1))
    return s


def extend(centre, rims):
    lanes = centre.shape[1]
    above = rims[:32].reshape(4, 1, 8, lanes)
    below = rims[32:].reshape(4, 1, 8, lanes)
    return jnp.concatenate([above, centre.reshape(4, 8, 8, lanes), below], axis=1).reshape(320, lanes)


def put_shifts(ext, dst, first_row):
    lanes = ext.shape[1]
    col = iota(ext.shape, 0) & 7
    for e in range(3):
        if e == 0:
            moved = jnp.where(col == 0, 0.0, pltpu.roll(ext, 1, 0))
        elif e == 1:
            moved = ext
        else:
            moved = jnp.where(col == 7, 0.0, pltpu.roll(ext, 319, 0))
        moved = moved.reshape(4, 10, 8, lanes)
        for b in range(3):
            dst[3 * b + e, first_row : first_row + 256, :] = moved[:, b : b + 8].reshape(256, lanes).astype(BF16)


def pack_stats(first, second):
    return jnp.concatenate([first[:, :128], first[:, 128:], second[:, :128], second[:, 128:], jnp.zeros((4, 128), F32)], axis=0)


def kernel(
    clip, rows, cols, start, feats, feats4, grads, grads4, wsh, gamma, beta, bias,
    conv_out, in_grad, wg_out,
    halo_x, halo_g, plane_st, z_st, plane_bk, z_bk,
    pair_w, zbuf, wall, hsh, gsh, gt, prod, s0buf, qsum, s1buf, rsum, s2buf, s3src, s3buf, s4src,
    acc_e, acc_o, acc_h, normed_s, dfac_s, stat_s,
    sem_halo, sem_st, sem_bk, sem_w, sem_rs,
):
    d, t = lax.axis_index("dp"), lax.axis_index("tile")
    y, xh = d // 2, d % 2
    z, xl, core = t // 4, (t // 2) % 2, t % 2
    x = xh * 2 + xl
    other = 1 - core

    def device(px, py, pz, pc):
        return (py * 2 + px // 2, pz * 4 + (px % 2) * 2 + pc)

    def first_peer(j):
        return device((x + j * core) % 4, (y + j * other) % 4, z, core)

    def second_peer(j):
        return device((x + j * other) % 4, (y + j * core) % 4, z, core)

    def z_peer(j):
        return device(x, y, (z + j) % 8, core)

    own_f = y * other + x * core
    own_s = x * other + y * core
    sibling = device(x, y, z, other)
    beside = device(xh * 2 + 1 - xl, y, z, core)
    diagonal = device(xh * 2 + 1 - xl, y, z, other)
    above_t, below_t = (t + 31) % 32, (t + 1) % 32

    def copy(src, dst, sems, k, target):
        return pltpu.make_async_remote_copy(
            src_ref=src, dst_ref=dst, send_sem=sems.at[0, k], recv_sem=sems.at[1, k],
            device_id=target, device_id_type=MESH,
        )

    barrier = pltpu.get_barrier_semaphore()
    peers = [sibling, diagonal, (d, above_t), (d, below_t)]
    peers += [z_peer(j) for j in range(1, 8)]
    peers += [first_peer(j) for j in (1, 2, 3)] + [second_peer(j) for j in (1, 2, 3)]
    for peer in peers:
        pl.semaphore_signal(barrier, inc=1, device_id=peer, device_id_type=MESH)

    own = clip[0, t]
    first = start[0, own]
    ncols = cols[0, own]
    nrows = rows[0, t]
    weights = [jnp.where(clip[0, k] == own, 1, 0) for k in range(32)]
    clip_rows = functools.reduce(lambda a, b: a + b, [weights[k] * rows[0, k] for k in range(32)])
    scale = 1.0 / (jnp.full((1, 128), (4 - first) * ncols * clip_rows * 6, I32).astype(F32))
    keep_above = jnp.where((t > 0) & (clip[0, above_t] == own) & (rows[0, above_t] > 7), 1, 0)
    keep_below = jnp.where((t < 31) & (clip[0, below_t] == own), 1, 0)

    n = iota((256, 128), 0)
    vmask = one_hot(((n >> 6) >= first) & (((n >> 3) & 7) < nrows) & ((n & 7) < ncols), F32)
    n = iota((64, 128), 0)
    keep = jnp.where(n < 32, keep_above, keep_below)
    rmask = one_hot((((n >> 3) & 3) >= first) & ((n & 7) < ncols) & (keep == 1), F32)
    vmask2, rmask2 = twice(vmask), twice(rmask)

    spread_in = one_hot(iota((192, 256), 0) == in_channel(iota((192, 256), 1)), BF16)
    masked = dot(feats[...], spread_in) * vmask2
    stats = pack_stats(jnp.sum(masked, axis=0, keepdims=True), jnp.sum(masked * masked, axis=0, keepdims=True))
    plane_st[xl * 2 + core] = stats
    pair_w[core] = wsh[core]

    pl.semaphore_wait(barrier, len(peers))

    pair_copy = copy(wsh.at[other], pair_w.at[core], sem_w, 0, sibling)
    pair_copy.start()

    def plane_send(buf, sems):
        q = xl * 2 + core
        out = [copy(buf.at[q], buf.at[q], sems, k, peer) for k, peer in enumerate((sibling, beside, diagonal))]
        for c in out:
            c.start()
        return out

    def z_send(plane, buf, sems, copies):
        for c in copies:
            c.wait_recv()
        buf[z] = jnp.concatenate([plane[q][:4] for q in range(4)], axis=0)
        out = [copy(buf.at[z], buf.at[z], sems, 2 + j, z_peer(j)) for j in range(1, 8)]
        for c in out:
            c.start()
        return out

    def clip_sums(buf, copies):
        for c in copies:
            c.wait_recv()
        row = iota((16, 128), 0) >> 2
        total = jnp.zeros((16, 128), F32)
        for k in range(8):
            w = [weights[4 * k + q] for q in range(4)]
            wrow = jnp.where(row == 0, w[0], jnp.where(row == 1, w[1], jnp.where(row == 2, w[2], w[3])))
            total = total + jnp.where(wrow == 1, buf[k], 0.0)
        total = group_sum(total[0:4] + total[4:8] + total[8:12] + total[12:16])
        halves = total * scale
        return (
            jnp.concatenate([halves[0:1], halves[1:2]], axis=1),
            jnp.concatenate([halves[2:3], halves[3:4]], axis=1),
        )

    st1 = plane_send(plane_st, sem_st)
    halos = [
        copy(feats4.at[:, 7], halo_x.at[0], sem_halo, 0, (d, below_t)),
        copy(feats4.at[:, 0], halo_x.at[1], sem_halo, 1, (d, above_t)),
        copy(grads4.at[:, 7], halo_g.at[0], sem_halo, 2, (d, below_t)),
        copy(grads4.at[:, 0], halo_g.at[1], sem_halo, 3, (d, above_t)),
    ]
    for c in halos:
        c.start()

    pair_copy.wait_recv()
    zbuf[z] = pair_w[...].reshape(16, 384).astype(BF16)
    zw = [copy(zbuf.at[z], zbuf.at[z], sem_w, j, z_peer(j)) for j in range(1, 8)]
    for c in zw:
        c.start()
    st2 = z_send(plane_st, z_st, sem_st, st1)

    hsh[:, 0:128, :] = jnp.zeros((9, 128, 256), BF16)
    gsh[:, 256:384, :] = jnp.zeros((9, 128, 384), BF16)
    spread_out = one_hot(iota((192, 384), 0) == out_channel(iota((192, 384), 1)), BF16)
    ge = dot(grads[...], spread_out) * jnp.concatenate([vmask, vmask, vmask], axis=1)
    get = ge.T.astype(BF16)
    gt[0:256] = get[0:256]
    gt[256:384] = get[0:128]
    gt[384:512] = get[256:384]
    halos[2].wait_recv()
    halos[3].wait_recv()
    gr = dot(halo_g[...].astype(F32).reshape(64, 192).astype(BF16), spread_out)
    put_shifts(extend(ge, gr * jnp.concatenate([rmask, rmask, rmask], axis=1)), gsh, 0)

    for c in zw:
        c.wait_recv()
    wall[core, own_f, own_s] = zbuf[...].astype(F32).reshape(128, 384).T[0:336].astype(BF16)
    w2 = [copy(wall.at[core, own_f, own_s], wall.at[core, own_f, own_s], sem_w, 7 + j, second_peer(j)) for j in (1, 2, 3)]
    for c in w2:
        c.start()

    mean, square = clip_sums(z_st, st2)
    inv_std = lax.rsqrt(square - mean * mean + EPSILON)
    spread_f32 = spread_in.astype(F32)
    gamma_l = exact_dot(gamma[...], spread_f32)
    beta_l = exact_dot(beta[...], spread_f32)
    normed = (masked - mean) * inv_std
    act = normed * gamma_l + beta_l
    sig = 1.0 / (1.0 + jnp.exp(-act))
    normed_s[...] = normed
    dfac_s[...] = vmask2 * sig * (1.0 + act * (1.0 - sig)) * gamma_l
    halos[0].wait_recv()
    halos[1].wait_recv()
    rim = dot(halo_x[...].astype(F32).reshape(64, 192).astype(BF16), spread_in)
    rim_act = (rim * rmask2 - mean) * inv_std * gamma_l + beta_l
    rim_hidden = rim_act / (1.0 + jnp.exp(-rim_act)) * rmask2
    put_shifts(extend(act * sig * vmask2, rim_hidden), hsh, 128)

    for c in w2:
        c.wait_recv()
    w3 = [copy(wall.at[core, own_f], wall.at[core, own_f], sem_w, 10 + j, first_peer(j)) for j in (1, 2, 3)]
    for c in w3:
        c.start()
    w4 = [copy(wall.at[core, own_f], wall.at[core, own_f], sem_w, 14, sibling)]
    w4[0].start()

    def tap_of(tap):
        tap = tap - tap // 27
        return tap // 9, tap % 9

    def hidden_tap(tap):
        a, be = tap_of(tap)
        return hsh[be, pl.ds(pl.multiple_of(a * 64, 64), 256), :]

    def product_half(h):
        def body(p, carry):
            ra = dot(gt[0:256], hidden_tap(h * 14 + 2 * p))
            rb = dot(gt[256:512], hidden_tap(h * 14 + 2 * p + 1))
            for kind, value in enumerate((ra[0:128], rb[0:128], ra[128:256] + rb[128:256])):
                value = value.astype(BF16)
                for dd in range(8):
                    for ll in range(2):
                        py, px = dd // 2, (dd % 2) * 2 + ll
                        f = py * (1 - h) + px * h
                        s = px * (1 - h) + py * h
                        prod[h, f, s, pl.ds(pl.multiple_of(p * 48 + kind * 16, 16), 16), :] = value[
                            dd * 16 : dd * 16 + 16, ll * 128 : ll * 128 + 128
                        ]
            return carry

        lax.fori_loop(0, 7, body, 0)

    product_half(other)
    s0 = copy(prod.at[other], s0buf, sem_rs, 0, sibling)
    s0.start()

    for j in (1, 2, 3):
        w3[j - 1].wait_recv()
        f = (own_f + 4 - j) % 4
        w4.append(copy(wall.at[core, f], wall.at[core, f], sem_w, 14 + j, sibling))
        w4[j].start()
    product_half(core)

    s0.wait_recv()

    def add_pair(k, carry):
        f, s = k // 4, k % 4
        qsum[f, s] = (prod[core, f, s].astype(F32) + s0buf[f, s].astype(F32)).astype(BF16)
        return carry

    lax.fori_loop(0, 16, add_pair, 0)
    s1 = [copy(qsum.at[(own_f + j) % 4], s1buf.at[j - 1], sem_rs, j, first_peer(j)) for j in (1, 2, 3)]
    for c in s1:
        c.start()

    acc_e[...] = jnp.zeros_like(acc_e)
    acc_o[...] = jnp.zeros_like(acc_o)
    acc_h[...] = jnp.zeros_like(acc_h)
    for c in w4:
        c.wait_recv()

    def conv_half(h):
        def tap_weight(p, kind):
            lanes = []
            for ll in range(2):
                parts = []
                for dd in range(8):
                    py, px = dd // 2, (dd % 2) * 2 + ll
                    f, s = (py, px) if h == 0 else (px, py)
                    parts.append(wall[h, f, s, pl.ds(pl.multiple_of(p * 48 + kind * 16, 16), 16), :])
                lanes.append(jnp.concatenate(parts, axis=0))
            return jnp.concatenate(lanes, axis=1)

        def grad_tap(tap, tail):
            a, be = tap_of(tap)
            rows_ = pl.ds(pl.multiple_of((2 - a) * 64, 64), 256)
            return jnp.concatenate([gsh[8 - be, rows_, 0:128], gsh[8 - be, rows_, 128 * tail : 128 * tail + 128]], axis=1)

        def body(p, carry):
            tap = h * 14 + 2 * p
            shared = tap_weight(p, 2)
            wa = jnp.concatenate([tap_weight(p, 0), shared], axis=0)
            wb = jnp.concatenate([tap_weight(p, 1), shared], axis=0)
            acc_h[...] += dot(grad_tap(tap, 1), wa) + dot(grad_tap(tap + 1, 2), wb)
            acc_e[...] += lax.dot_general(hidden_tap(tap), wa, NT_DIMS, preferred_element_type=F32)
            acc_o[...] += lax.dot_general(hidden_tap(tap + 1), wb, NT_DIMS, preferred_element_type=F32)
            return carry

        lax.fori_loop(0, 7, body, 0)

    conv_half(0)
    conv_half(1)

    dn = acc_h[...] * dfac_s[...]
    back = pack_stats(jnp.sum(dn, axis=0, keepdims=True), jnp.sum(dn * normed_s[...], axis=0, keepdims=True))
    acc_h[...] = dn
    plane_bk[xl * 2 + core] = back
    bk1 = plane_send(plane_bk, sem_bk)

    lane256 = iota((256, 192), 0)
    pack_out = one_hot(jnp.where(lane256 < 128, out_channel(lane256), jnp.where((lane256 & 15) < 8, out_channel(lane256), -1)) == iota((256, 192), 1), BF16)
    bias_l = exact_dot(bias[...], spread_out[:, 0:256].astype(F32))
    tail_odd = pltpu.roll(acc_o[:, 128:256], 120, 1)
    conv = jnp.concatenate([acc_e[:, 0:128] + acc_o[:, 0:128], acc_e[:, 128:256] + tail_odd], axis=1)
    conv = ((conv + bias_l) * vmask2).astype(BF16)
    conv_out[...] = dot(conv, pack_out).astype(BF16)
    bk2 = z_send(plane_bk, z_bk, sem_bk, bk1)

    for c in s1:
        c.wait_recv()

    def add_first(s, carry):
        total = qsum[own_f, s].astype(F32)
        for j in range(3):
            total = total + s1buf[j, s].astype(F32)
        rsum[s] = total.astype(BF16)
        return carry

    lax.fori_loop(0, 4, add_first, 0)
    s2 = [copy(rsum.at[(own_s + j) % 4], s2buf.at[j - 1], sem_rs, 3 + j, second_peer(j)) for j in (1, 2, 3)]
    for c in s2:
        c.start()

    sum_one, sum_two = clip_sums(z_bk, bk2)
    pack_in = one_hot(in_channel(iota((256, 192), 0)) == iota((256, 192), 1), BF16)
    grad_x = inv_std * (acc_h[...] - sum_one - normed_s[...] * sum_two) * vmask2
    in_grad[...] = dot(grad_x.astype(BF16), pack_in).astype(BF16)

    for c in s2:
        c.wait_recv()
    total = rsum[own_s].astype(F32)
    for j in range(3):
        total = total + s2buf[j].astype(F32)
    total = jnp.concatenate([total, jnp.zeros((48, 128), F32)], axis=0).T
    s3src[...] = total.reshape(8, 16, 384).astype(BF16)
    s3 = [copy(s3src.at[(z + j) % 8], s3buf.at[j - 1], sem_rs, 6 + j, z_peer(j)) for j in range(1, 8)]
    for c in s3:
        c.start()
    for c in s3:
        c.wait_recv()
    total = s3src[z].astype(F32)
    for j in range(7):
        total = total + s3buf[j].astype(F32)
    s4src[...] = total.reshape(2, 8, 384)
    s4 = copy(s4src.at[other], stat_s, sem_rs, 14, sibling)
    s4.start()
    s4.wait_recv()
    wg_out[core] = s4src[core]
    wg_out[other] = stat_s[...]
    for c in [pair_copy, s0, s4] + zw + w2 + w3 + w4 + s1 + s2 + s3 + st1 + st2 + bk1 + bk2 + halos:
        c.wait_send()


def on_device(features, out_grad, weight, bias, gamma, beta, tile_clip, tile_rows, clip_cols, clip_start):
    w = jnp.pad(weight.astype(F32), ((0, 2), (0, 1), (0, 0))).reshape(8, 14, 2, 24)
    w = jnp.concatenate([w[..., :16].reshape(8, 14, 32), w[..., 16:].reshape(8, 14, 16)], axis=-1)
    w = jnp.pad(w.reshape(8, 2, 336).transpose(1, 0, 2), ((0, 0), (0, 0), (0, 48)))
    dma = pltpu.SemaphoreType.DMA
    vmem, smem = pl.BlockSpec(memory_space=pltpu.VMEM), pl.BlockSpec(memory_space=pltpu.SMEM)
    conv_out, in_grad, wg = pl.pallas_call(
        kernel,
        out_shape=(
            jax.ShapeDtypeStruct((256, 192), BF16),
            jax.ShapeDtypeStruct((256, 192), BF16),
            jax.ShapeDtypeStruct((2, 8, 384), F32),
        ),
        in_specs=[smem] * 4 + [vmem] * 8,
        out_specs=[vmem] * 3,
        scratch_shapes=[
            pltpu.VMEM((2, 4, 8, 192), BF16),
            pltpu.VMEM((2, 4, 8, 192), BF16),
            pltpu.VMEM((4, 8, 128), F32),
            pltpu.VMEM((8, 16, 128), F32),
            pltpu.VMEM((4, 8, 128), F32),
            pltpu.VMEM((8, 16, 128), F32),
            pltpu.VMEM((2, 8, 384), F32),
            pltpu.VMEM((8, 16, 384), BF16),
            pltpu.VMEM((2, 4, 4, 336, 128), BF16),
            pltpu.VMEM((9, 384, 256), BF16),
            pltpu.VMEM((9, 384, 384), BF16),
            pltpu.VMEM((512, 256), BF16),
            pltpu.VMEM((2, 4, 4, 336, 128), BF16),
            pltpu.VMEM((4, 4, 336, 128), BF16),
            pltpu.VMEM((4, 4, 336, 128), BF16),
            pltpu.VMEM((3, 4, 336, 128), BF16),
            pltpu.VMEM((4, 336, 128), BF16),
            pltpu.VMEM((3, 336, 128), BF16),
            pltpu.VMEM((8, 16, 384), BF16),
            pltpu.VMEM((7, 16, 384), BF16),
            pltpu.VMEM((2, 8, 384), F32),
            pltpu.VMEM((256, 256), F32),
            pltpu.VMEM((256, 256), F32),
            pltpu.VMEM((256, 256), F32),
            pltpu.VMEM((256, 256), F32),
            pltpu.VMEM((256, 256), F32),
            pltpu.VMEM((8, 384), F32),
            dma((2, 4)),
            dma((2, 10)),
            dma((2, 10)),
            dma((2, 18)),
            dma((2, 15)),
        ],
        compiler_params=pltpu.CompilerParams(collective_id=0, has_side_effects=True, vmem_limit_bytes=56 * 1024 * 1024),
    )(
        tile_clip, tile_rows, clip_cols, clip_start,
        features.reshape(256, 192), features.reshape(4, 8, 8, 192),
        out_grad.reshape(256, 192), out_grad.reshape(4, 8, 8, 192),
        w, gamma.reshape(1, 192), beta.reshape(1, 192), bias.reshape(1, 192),
    )
    wg = wg[:, :6, :336].transpose(1, 0, 2).reshape(6, 14, 48)
    wg = jnp.concatenate([wg[..., :32].reshape(6, 14, 2, 16), wg[..., 32:].reshape(6, 14, 2, 8)], axis=-1)
    wg = wg.reshape(6, 28, 24)[:, :27]
    return (conv_out.reshape(features.shape), in_grad.reshape(features.shape), wg)


def solution(mesh):
    in_specs = (
        P("dp", None, "tile", None, None),
        P("dp", None, "tile", None, None),
        P("tile", None, "dp"),
        P(),
        P(),
        P(),
        P("dp", None),
        P("dp", None),
        P("dp", None),
        P("dp", None),
    )
    out_specs = (
        P("dp", None, "tile", None, None),
        P("dp", None, "tile", None, None),
        P("tile", None, "dp"),
    )
    return jax.shard_map(on_device, mesh=mesh, in_specs=in_specs, out_specs=out_specs, check_vma=False)
```

```python
import functools

import jax
import jax.numpy as jnp
from jax import lax
from jax.experimental import pallas as pl
from jax.experimental.pallas import tpu as pltpu
from jax.sharding import PartitionSpec as P


MESH = pl.DeviceIdType.MESH
F32, BF16, I32 = jnp.float32, jnp.bfloat16, jnp.int32
EPSILON = 1e-05
NT_DIMS = (((1,), (1,)), ((), ()))


def iota(shape, dim):
    return lax.broadcasted_iota(I32, shape, dim)


def in_channel(lane):
    group, r = (((lane >> 4) & 7) * 4 + (lane >> 7) * 2 + ((lane >> 3) & 1)), lane & 7
    return jnp.where(r < 6, group * 6 + r, -1)


def out_channel(lane):
    kind, m = lane >> 7, lane & 127
    d, j = m >> 4, m & 15
    tail = jnp.where(kind == 1, jnp.where(j < 8, d * 24 + 16 + j, -1), jnp.where(j >= 8, d * 24 + 8 + j, -1))
    return jnp.where(kind == 0, d * 24 + j, tail)


def one_hot(equal, dtype):
    return jnp.where(equal, 1.0, 0.0).astype(dtype)


def dot(a, b):
    return jnp.dot(a, b, preferred_element_type=F32)


def exact_dot(a, b):
    return jnp.dot(a, b, preferred_element_type=F32, precision=lax.Precision.HIGHEST)


def twice(mask):
    return jnp.concatenate([mask, mask], axis=1)


def group_sum(s):
    lane = iota(s.shape, 1)
    for shift in (1, 2, 4):
        s = s + jnp.where((lane & shift) != 0, pltpu.roll(s, shift, 1), pltpu.roll(s, 128 - shift, 1))
    return s


def extend(centre, rims):
    lanes = centre.shape[1]
    above = rims[:32].reshape(4, 1, 8, lanes)
    below = rims[32:].reshape(4, 1, 8, lanes)
    return jnp.concatenate([above, centre.reshape(4, 8, 8, lanes), below], axis=1).reshape(320, lanes)


def put_shifts(ext, dst, first_row):
    lanes = ext.shape[1]
    col = iota(ext.shape, 0) & 7
    for e in range(3):
        if e == 0:
            moved = jnp.where(col == 0, 0.0, pltpu.roll(ext, 1, 0))
        elif e == 1:
            moved = ext
        else:
            moved = jnp.where(col == 7, 0.0, pltpu.roll(ext, 319, 0))
        moved = moved.reshape(4, 10, 8, lanes)
        for b in range(3):
            dst[3 * b + e, first_row : first_row + 256, :] = moved[:, b : b + 8].reshape(256, lanes).astype(BF16)


def place(lane):
    u, j = lane >> 4, lane & 15
    p = (u * 171) >> 9
    kind = u - 3 * p
    tap = 2 * p + jnp.where(kind == 2, j >> 3, kind)
    return jnp.where(lane < 336, tap, -64), jnp.where(kind == 2, 16 + (j & 7), j)


def pack_stats(first, second):
    return jnp.concatenate([first[:, :128], first[:, 128:], second[:, :128], second[:, 128:], jnp.zeros((4, 128), F32)], axis=0)


def kernel(
    clip, rows, cols, start, feats, feats4, grads, grads4, weight, gamma, beta, bias,
    conv_out, in_grad, wg_out,
    halo_x, halo_g, plane_st, z_st, plane_bk, z_bk,
    wsh, sel_s, pair_w, zbuf, wall, hsh, gsh, gt, prod, s0buf, qsum, s1a, s1b, rsum, s2buf, s3own, s3src, s3buf, s4src,
    acc_e, acc_o, acc_h, normed_s, dfac_s, stat_s,
    sem_halo, sem_st, sem_bk, sem_w, sem_rs,
):
    d, t = lax.axis_index("dp"), lax.axis_index("tile")
    y, xh = d // 2, d % 2
    z, xl, core = t // 4, (t // 2) % 2, t % 2
    x = xh * 2 + xl
    other = 1 - core

    def device(px, py, pz, pc):
        return (py * 2 + px // 2, pz * 4 + (px % 2) * 2 + pc)

    def first_peer(j):
        return device((x + j * core) % 4, (y + j * other) % 4, z, core)

    def second_peer(j):
        return device((x + j * other) % 4, (y + j * core) % 4, z, core)

    def z_peer(j):
        return device(x, y, (z + j) % 8, core)

    own_f = y * other + x * core
    own_s = x * other + y * core
    sibling = device(x, y, z, other)
    beside = device(xh * 2 + 1 - xl, y, z, core)
    diagonal = device(xh * 2 + 1 - xl, y, z, other)
    above_t, below_t = (t + 31) % 32, (t + 1) % 32

    def copy(src, dst, sems, k, target):
        return pltpu.make_async_remote_copy(
            src_ref=src, dst_ref=dst, send_sem=sems.at[0, k], recv_sem=sems.at[1, k],
            device_id=target, device_id_type=MESH,
        )

    barrier = pltpu.get_barrier_semaphore()
    peers = [sibling, diagonal, (d, above_t), (d, below_t)]
    peers += [z_peer(j) for j in range(1, 8)]
    peers += [first_peer(j) for j in (1, 2, 3)] + [second_peer(j) for j in (1, 2, 3)]
    for peer in peers:
        pl.semaphore_signal(barrier, inc=1, device_id=peer, device_id_type=MESH)

    own = clip[0, t]
    first = start[0, own]
    ncols = cols[0, own]
    nrows = rows[0, t]
    weights = [jnp.where(clip[0, k] == own, 1, 0) for k in range(32)]
    clip_rows = functools.reduce(lambda a, b: a + b, [weights[k] * rows[0, k] for k in range(32)])
    scale = 1.0 / (jnp.full((1, 128), (4 - first) * ncols * clip_rows * 6, I32).astype(F32))
    keep_above = jnp.where((t > 0) & (clip[0, above_t] == own) & (rows[0, above_t] > 7), 1, 0)
    keep_below = jnp.where((t < 31) & (clip[0, below_t] == own), 1, 0)

    n = iota((256, 128), 0)
    vmask = one_hot(((n >> 6) >= first) & (((n >> 3) & 7) < nrows) & ((n & 7) < ncols), F32)
    n = iota((64, 128), 0)
    keep = jnp.where(n < 32, keep_above, keep_below)
    rmask = one_hot((((n >> 3) & 3) >= first) & ((n & 7) < ncols) & (keep == 1), F32)
    vmask2, rmask2 = twice(vmask), twice(rmask)

    spread_in = one_hot(iota((192, 256), 0) == in_channel(iota((192, 256), 1)), BF16)
    masked = dot(feats[...], spread_in) * vmask2
    stats = pack_stats(jnp.sum(masked, axis=0, keepdims=True), jnp.sum(masked * masked, axis=0, keepdims=True))
    plane_st[xl * 2 + core] = stats

    tap_lane, out_lane = place(iota((27, 384), 1))
    for h in range(2):
        sel_s[h] = one_hot(tap_lane + 14 * h == iota((27, 384), 0), BF16)
    out_mask = one_hot(place(iota((24, 384), 1))[1] == iota((24, 384), 0), F32)
    flat = weight[...].astype(F32).reshape(144, 27).astype(BF16)
    for h in range(2):
        spread = dot(flat, sel_s[h]).reshape(6, 24, 384) * out_mask[None]
        wsh[h] = jnp.concatenate([jnp.sum(spread, axis=1), jnp.zeros((2, 384), F32)], axis=0)
    pair_w[core] = wsh[core]

    pl.semaphore_wait(barrier, len(peers))

    pair_copy = copy(wsh.at[other], pair_w.at[core], sem_w, 0, sibling)
    pair_copy.start()

    def plane_send(buf, sems):
        q = xl * 2 + core
        out = [copy(buf.at[q], buf.at[q], sems, k, peer) for k, peer in enumerate((sibling, beside, diagonal))]
        for c in out:
            c.start()
        return out

    def z_send(plane, buf, sems, copies):
        for c in copies:
            c.wait_recv()
        buf[z] = jnp.concatenate([plane[q][:4] for q in range(4)], axis=0)
        out = [copy(buf.at[z], buf.at[z], sems, 2 + j, z_peer(j)) for j in range(1, 8)]
        for c in out:
            c.start()
        return out

    def clip_sums(buf, copies):
        for c in copies:
            c.wait_recv()
        row = iota((16, 128), 0) >> 2
        total = jnp.zeros((16, 128), F32)
        for k in range(8):
            w = [weights[4 * k + q] for q in range(4)]
            wrow = jnp.where(row == 0, w[0], jnp.where(row == 1, w[1], jnp.where(row == 2, w[2], w[3])))
            total = total + jnp.where(wrow == 1, buf[k], 0.0)
        total = group_sum(total[0:4] + total[4:8] + total[8:12] + total[12:16])
        halves = total * scale
        return (
            jnp.concatenate([halves[0:1], halves[1:2]], axis=1),
            jnp.concatenate([halves[2:3], halves[3:4]], axis=1),
        )

    st1 = plane_send(plane_st, sem_st)
    halos = [
        copy(feats4.at[:, 7], halo_x.at[0], sem_halo, 0, (d, below_t)),
        copy(feats4.at[:, 0], halo_x.at[1], sem_halo, 1, (d, above_t)),
        copy(grads4.at[:, 7], halo_g.at[0], sem_halo, 2, (d, below_t)),
        copy(grads4.at[:, 0], halo_g.at[1], sem_halo, 3, (d, above_t)),
    ]
    for c in halos:
        c.start()

    pair_copy.wait_recv()
    zbuf[z] = pair_w[...].reshape(16, 384).astype(BF16)
    zw = [copy(zbuf.at[z], zbuf.at[z], sem_w, j, z_peer(j)) for j in range(1, 8)]
    for c in zw:
        c.start()
    st2 = z_send(plane_st, z_st, sem_st, st1)

    hsh[:, 0:128, :] = jnp.zeros((9, 128, 256), BF16)
    gsh[:, 256:384, :] = jnp.zeros((9, 128, 384), BF16)
    spread_out = one_hot(iota((192, 384), 0) == out_channel(iota((192, 384), 1)), BF16)
    ge = dot(grads[...], spread_out) * jnp.concatenate([vmask, vmask, vmask], axis=1)
    get = ge.T.astype(BF16)
    gt[0:256] = get[0:256]
    gt[256:384] = get[0:128]
    gt[384:512] = get[256:384]
    halos[2].wait_recv()
    halos[3].wait_recv()
    gr = dot(halo_g[...].astype(F32).reshape(64, 192).astype(BF16), spread_out)
    put_shifts(extend(ge, gr * jnp.concatenate([rmask, rmask, rmask], axis=1)), gsh, 0)

    for c in zw:
        c.wait_recv()
    wall[core, own_f, own_s] = zbuf[...].astype(F32).reshape(128, 384).T[0:336].astype(BF16)
    w2 = [copy(wall.at[core, own_f, own_s], wall.at[core, own_f, own_s], sem_w, 7 + j, second_peer(j)) for j in (1, 2, 3)]
    for c in w2:
        c.start()

    mean, square = clip_sums(z_st, st2)
    inv_std = lax.rsqrt(square - mean * mean + EPSILON)
    spread_f32 = spread_in.astype(F32)
    gamma_l = exact_dot(gamma[...], spread_f32)
    beta_l = exact_dot(beta[...], spread_f32)
    normed = (masked - mean) * inv_std
    act = normed * gamma_l + beta_l
    sig = 1.0 / (1.0 + jnp.exp(-act))
    normed_s[...] = normed
    dfac_s[...] = vmask2 * sig * (1.0 + act * (1.0 - sig)) * gamma_l
    halos[0].wait_recv()
    halos[1].wait_recv()
    rim = dot(halo_x[...].astype(F32).reshape(64, 192).astype(BF16), spread_in)
    rim_act = (rim * rmask2 - mean) * inv_std * gamma_l + beta_l
    rim_hidden = rim_act / (1.0 + jnp.exp(-rim_act)) * rmask2
    put_shifts(extend(act * sig * vmask2, rim_hidden), hsh, 128)

    def tap_of(tap):
        tap = tap - tap // 27
        return tap // 9, tap % 9

    def hidden_tap(tap):
        a, be = tap_of(tap)
        return hsh[be, pl.ds(pl.multiple_of(a * 64, 64), 256), :]

    def piece(h, dd, ll):
        py, px = dd // 2, (dd % 2) * 2 + ll
        return py * (1 - h) + px * h, px * (1 - h) + py * h

    def strip(p, kind):
        return pl.ds(pl.multiple_of(p * 48 + kind * 16, 16), 16)

    def product(h, low, high, final):
        def body(p, carry):
            ra = dot(gt[0:256], hidden_tap(h * 14 + 2 * p))
            rb = dot(gt[256:512], hidden_tap(h * 14 + 2 * p + 1))
            for kind, value in enumerate((ra[0:128], rb[0:128], ra[128:256] + rb[128:256])):
                for dd in range(8):
                    for ll in range(2):
                        f, s = piece(h, dd, ll)
                        tile = value[dd * 16 : dd * 16 + 16, ll * 128 : ll * 128 + 128]
                        if final:
                            qsum[f, s, strip(p, kind), :] = (tile + s0buf[f, s, strip(p, kind), :].astype(F32)).astype(BF16)
                        else:
                            prod[f, s, strip(p, kind), :] = tile.astype(BF16)
            return carry

        lax.fori_loop(low, high, body, 0)

    chunks = ((0, 4), (4, 7))
    spans = [pl.ds(48 * low, 48 * (high - low)) for low, high in chunks]
    every = pl.ds(0, 4)
    s0 = []
    for k, (low, high) in enumerate(chunks):
        product(other, low, high, False)
        s0.append(copy(prod.at[every, every, spans[k]], s0buf.at[every, every, spans[k]], sem_rs, k, sibling))
        s0[k].start()

    next_f, far_f, last_f = (own_f + 1) % 4, (own_f + 2) % 4, (own_f + 3) % 4
    left, right = pl.ds(0, 2), pl.ds(2, 2)

    def wcopy(f, part, k, target):
        return copy(wall.at[core, f, part], wall.at[core, f, part], sem_w, k, target)

    for c in w2:
        c.wait_recv()
    w3 = [
        wcopy(own_f, left, 11, first_peer(1)), wcopy(own_f, right, 12, first_peer(3)),
        wcopy(own_f, right, 13, first_peer(1)), wcopy(own_f, left, 14, first_peer(3)),
    ]
    for c in w3:
        c.start()
    w4 = [wcopy(own_f, every, 17, sibling)]
    w4[0].start()

    s1 = []
    for k, (low, high) in enumerate(chunks):
        s0[k].wait_recv()
        product(core, low, high, True)
        s1.append([
            copy(qsum.at[far_f, left, spans[k]], s1a.at[0, left, spans[k]], sem_rs, 2 + 2 * k, first_peer(1)),
            copy(qsum.at[far_f, right, spans[k]], s1a.at[1, left, spans[k]], sem_rs, 3 + 2 * k, first_peer(3)),
        ])
        for c in s1[k]:
            c.start()

    w3[0].wait_recv()
    w5 = [wcopy(last_f, left, 15, first_peer(1))]
    w5[0].start()
    w3[1].wait_recv()
    w5.append(wcopy(next_f, right, 16, first_peer(3)))
    w5[1].start()

    s1n = []
    for k in range(2):
        for c in s1[k]:
            c.wait_recv()
        for s in range(2):
            qsum[next_f, s, spans[k]] = (qsum[next_f, s, spans[k]].astype(F32) + s1a[0, s, spans[k]].astype(F32)).astype(BF16)
            qsum[last_f, 2 + s, spans[k]] = (qsum[last_f, 2 + s, spans[k]].astype(F32) + s1a[1, s, spans[k]].astype(F32)).astype(BF16)
        s1n.append([
            copy(qsum.at[next_f, every, spans[k]], s1b.at[0, every, spans[k]], sem_rs, 6 + 2 * k, first_peer(1)),
            copy(qsum.at[last_f, every, spans[k]], s1b.at[1, every, spans[k]], sem_rs, 7 + 2 * k, first_peer(3)),
        ])
        for c in s1n[k]:
            c.start()

    w3[2].wait_recv()
    w4.append(wcopy(last_f, every, 18, sibling))
    w4[1].start()
    w3[3].wait_recv()
    w4.append(wcopy(next_f, every, 19, sibling))
    w4[2].start()
    for c in w5:
        c.wait_recv()
    w4.append(wcopy(far_f, every, 20, sibling))
    w4[3].start()

    def tap_weight(h, p, kind):
        lanes = []
        for ll in range(2):
            parts = []
            for dd in range(8):
                f, s = piece(h, dd, ll)
                parts.append(wall[h, f, s, strip(p, kind), :])
            lanes.append(jnp.concatenate(parts, axis=0))
        return jnp.concatenate(lanes, axis=1)

    def tap_weights(h, p):
        shared = tap_weight(h, p, 2)
        return [jnp.concatenate([tap_weight(h, p, kind), shared], axis=0) for kind in range(2)]

    def grad_tap(tap, tail):
        a, be = tap_of(tap)
        rows_ = pl.ds(pl.multiple_of((2 - a) * 64, 64), 256)
        return jnp.concatenate([gsh[8 - be, rows_, 0:128], gsh[8 - be, rows_, 128 * tail : 128 * tail + 128]], axis=1)

    def hidden_half(h):
        def body(p, carry):
            tap = h * 14 + 2 * p
            wa, wb = tap_weights(h, p)
            acc_h[...] += dot(grad_tap(tap, 1), wa) + dot(grad_tap(tap + 1, 2), wb)
            return carry

        lax.fori_loop(0, 7, body, 0)

    def conv_half(h):
        def body(p, carry):
            tap = h * 14 + 2 * p
            wa, wb = tap_weights(h, p)
            acc_e[...] += lax.dot_general(hidden_tap(tap), wa, NT_DIMS, preferred_element_type=F32)
            acc_o[...] += lax.dot_general(hidden_tap(tap + 1), wb, NT_DIMS, preferred_element_type=F32)
            return carry

        lax.fori_loop(0, 7, body, 0)

    acc_h[...] = jnp.zeros_like(acc_h)
    hidden_half(core)
    for c in w4:
        c.wait_recv()
    hidden_half(other)

    dn = acc_h[...] * dfac_s[...]
    back = pack_stats(jnp.sum(dn, axis=0, keepdims=True), jnp.sum(dn * normed_s[...], axis=0, keepdims=True))
    acc_h[...] = dn
    plane_bk[xl * 2 + core] = back
    bk1 = plane_send(plane_bk, sem_bk)

    for pair in s1n:
        for c in pair:
            c.wait_recv()

    def first_total(s):
        return qsum[own_f, s].astype(F32) + s1b[0, s].astype(F32) + s1b[1, s].astype(F32)

    def add_first(s, carry):
        rsum[s] = first_total(s).astype(BF16)
        return carry

    lax.fori_loop(0, 4, add_first, 0)
    s2 = [copy(rsum.at[(own_s + j) % 4], s2buf.at[j - 1], sem_rs, 9 + j, second_peer(j)) for j in (1, 2, 3)]
    for c in s2:
        c.start()
    bk2 = z_send(plane_bk, z_bk, sem_bk, bk1)

    acc_e[...] = jnp.zeros_like(acc_e)
    acc_o[...] = jnp.zeros_like(acc_o)
    conv_half(core)
    conv_half(other)

    for c in s2:
        c.wait_recv()
    total = first_total(own_s)
    for j in range(3):
        total = total + s2buf[j].astype(F32)
    total = jnp.concatenate([total, jnp.zeros((48, 128), F32)], axis=0).T.reshape(8, 16, 384)
    s3own[...] = total
    s3src[...] = total.astype(BF16)
    s3 = [copy(s3src.at[(z + j) % 8], s3buf.at[j - 1], sem_rs, 12 + j, z_peer(j)) for j in range(1, 8)]
    for c in s3:
        c.start()

    lane256 = iota((256, 192), 0)
    pack_out = one_hot(jnp.where(lane256 < 128, out_channel(lane256), jnp.where((lane256 & 15) < 8, out_channel(lane256), -1)) == iota((256, 192), 1), BF16)
    bias_l = exact_dot(bias[...], spread_out[:, 0:256].astype(F32))
    tail_odd = pltpu.roll(acc_o[:, 128:256], 120, 1)
    conv = jnp.concatenate([acc_e[:, 0:128] + acc_o[:, 0:128], acc_e[:, 128:256] + tail_odd], axis=1)
    conv = ((conv + bias_l) * vmask2).astype(BF16)
    conv_out[...] = dot(conv, pack_out).astype(BF16)

    sum_one, sum_two = clip_sums(z_bk, bk2)
    pack_in = one_hot(in_channel(iota((256, 192), 0)) == iota((256, 192), 1), BF16)
    grad_x = inv_std * (acc_h[...] - sum_one - normed_s[...] * sum_two) * vmask2
    in_grad[...] = dot(grad_x.astype(BF16), pack_in).astype(BF16)

    for c in s3:
        c.wait_recv()
    total = s3own[z]
    for j in range(7):
        total = total + s3buf[j].astype(F32)
    s4src[...] = total.reshape(2, 8, 384)
    s4 = copy(s4src.at[other], stat_s, sem_rs, 20, sibling)
    s4.start()

    def unpack(value, h):
        flat = (value[0:6].reshape(6, 1, 384) * out_mask[None]).reshape(144, 384)
        high = flat.astype(BF16)
        low = (flat - high.astype(F32)).astype(BF16)
        return sum(lax.dot_general(v, sel_s[h], NT_DIMS, preferred_element_type=F32) for v in (high, low))

    own_part = unpack(s4src[core], core)
    s4.wait_recv()
    wg_out[...] = (own_part + unpack(stat_s[...], other)).reshape(6, 24, 27)
    for c in [pair_copy, s4] + zw + w2 + w3 + w4 + w5 + s0 + s1[0] + s1[1] + s1n[0] + s1n[1] + s2 + s3 + st1 + st2 + bk1 + bk2 + halos:
        c.wait_send()


def on_device(features, out_grad, weight, bias, gamma, beta, tile_clip, tile_rows, clip_cols, clip_start):
    dma = pltpu.SemaphoreType.DMA
    vmem, smem = pl.BlockSpec(memory_space=pltpu.VMEM), pl.BlockSpec(memory_space=pltpu.SMEM)
    conv_out, in_grad, wg = pl.pallas_call(
        kernel,
        out_shape=(
            jax.ShapeDtypeStruct((256, 192), BF16),
            jax.ShapeDtypeStruct((256, 192), BF16),
            jax.ShapeDtypeStruct((6, 24, 27), F32),
        ),
        in_specs=[smem] * 4 + [vmem] * 8,
        out_specs=[vmem] * 3,
        scratch_shapes=[
            pltpu.VMEM((2, 4, 8, 192), BF16),
            pltpu.VMEM((2, 4, 8, 192), BF16),
            pltpu.VMEM((4, 8, 128), F32),
            pltpu.VMEM((8, 16, 128), F32),
            pltpu.VMEM((4, 8, 128), F32),
            pltpu.VMEM((8, 16, 128), F32),
            pltpu.VMEM((2, 8, 384), F32),
            pltpu.VMEM((2, 27, 384), BF16),
            pltpu.VMEM((2, 8, 384), F32),
            pltpu.VMEM((8, 16, 384), BF16),
            pltpu.VMEM((2, 4, 4, 336, 128), BF16),
            pltpu.VMEM((9, 384, 256), BF16),
            pltpu.VMEM((9, 384, 384), BF16),
            pltpu.VMEM((512, 256), BF16),
            pltpu.VMEM((4, 4, 336, 128), BF16),
            pltpu.VMEM((4, 4, 336, 128), BF16),
            pltpu.VMEM((4, 4, 336, 128), BF16),
            pltpu.VMEM((2, 2, 336, 128), BF16),
            pltpu.VMEM((2, 4, 336, 128), BF16),
            pltpu.VMEM((4, 336, 128), BF16),
            pltpu.VMEM((3, 336, 128), BF16),
            pltpu.VMEM((8, 16, 384), F32),
            pltpu.VMEM((8, 16, 384), BF16),
            pltpu.VMEM((7, 16, 384), BF16),
            pltpu.VMEM((2, 8, 384), F32),
            pltpu.VMEM((256, 256), F32),
            pltpu.VMEM((256, 256), F32),
            pltpu.VMEM((256, 256), F32),
            pltpu.VMEM((256, 256), F32),
            pltpu.VMEM((256, 256), F32),
            pltpu.VMEM((8, 384), F32),
            dma((2, 4)),
            dma((2, 10)),
            dma((2, 10)),
            dma((2, 21)),
            dma((2, 21)),
        ],
        compiler_params=pltpu.CompilerParams(collective_id=0, has_side_effects=True, vmem_limit_bytes=56 * 1024 * 1024),
    )(
        tile_clip, tile_rows, clip_cols, clip_start,
        features.reshape(256, 192), features.reshape(4, 8, 8, 192),
        out_grad.reshape(256, 192), out_grad.reshape(4, 8, 8, 192),
        weight.transpose(0, 2, 1), gamma.reshape(1, 192), beta.reshape(1, 192), bias.reshape(1, 192),
    )
    return (conv_out.reshape(features.shape), in_grad.reshape(features.shape), wg.transpose(0, 2, 1))


def solution(mesh):
    in_specs = (
        P("dp", None, "tile", None, None),
        P("dp", None, "tile", None, None),
        P("tile", None, "dp"),
        P(),
        P(),
        P(),
        P("dp", None),
        P("dp", None),
        P("dp", None),
        P("dp", None),
    )
    out_specs = (
        P("dp", None, "tile", None, None),
        P("dp", None, "tile", None, None),
        P("tile", None, "dp"),
    )
    return jax.shard_map(on_device, mesh=mesh, in_specs=in_specs, out_specs=out_specs, check_vma=False)
```

```python
import functools

import jax
import jax.numpy as jnp
from jax import lax
from jax.experimental import pallas as pl
from jax.experimental.pallas import tpu as pltpu
from jax.sharding import PartitionSpec as P


MESH = pl.DeviceIdType.MESH
F32, BF16, I32 = jnp.float32, jnp.bfloat16, jnp.int32
EPSILON = 1e-05
NT_DIMS = (((1,), (1,)), ((), ()))


def iota(shape, dim):
    return lax.broadcasted_iota(I32, shape, dim)


def in_channel(lane):
    group, r = (((lane >> 4) & 7) * 4 + (lane >> 7) * 2 + ((lane >> 3) & 1)), lane & 7
    return jnp.where(r < 6, group * 6 + r, -1)


def out_channel(lane):
    kind, m = lane >> 7, lane & 127
    d, j = m >> 4, m & 15
    tail = jnp.where(kind == 1, jnp.where(j < 8, d * 24 + 16 + j, -1), jnp.where(j >= 8, d * 24 + 8 + j, -1))
    return jnp.where(kind == 0, d * 24 + j, tail)


def one_hot(equal, dtype):
    return jnp.where(equal, 1.0, 0.0).astype(dtype)


def dot(a, b):
    return jnp.dot(a, b, preferred_element_type=F32)


def exact_dot(a, b):
    return jnp.dot(a, b, preferred_element_type=F32, precision=lax.Precision.HIGHEST)


def twice(mask):
    return jnp.concatenate([mask, mask], axis=1)


def group_sum(s):
    lane = iota(s.shape, 1)
    for shift in (1, 2, 4):
        s = s + jnp.where((lane & shift) != 0, pltpu.roll(s, shift, 1), pltpu.roll(s, 128 - shift, 1))
    return s


def extend(centre, rims):
    lanes = centre.shape[1]
    above = rims[:32].reshape(4, 1, 8, lanes)
    below = rims[32:].reshape(4, 1, 8, lanes)
    return jnp.concatenate([above, centre.reshape(4, 8, 8, lanes), below], axis=1).reshape(320, lanes)


def put_shifts(ext, dst, first_row):
    lanes = ext.shape[1]
    col = iota(ext.shape, 0) & 7
    for e in range(3):
        if e == 0:
            moved = jnp.where(col == 0, 0.0, pltpu.roll(ext, 1, 0))
        elif e == 1:
            moved = ext
        else:
            moved = jnp.where(col == 7, 0.0, pltpu.roll(ext, 319, 0))
        moved = moved.reshape(4, 10, 8, lanes)
        for b in range(3):
            dst[3 * b + e, first_row : first_row + 256, :] = moved[:, b : b + 8].reshape(256, lanes).astype(BF16)


def place(lane):
    u, j = lane >> 4, lane & 15
    p = (u * 171) >> 9
    kind = u - 3 * p
    tap = 2 * p + jnp.where(kind == 2, j >> 3, kind)
    return jnp.where(lane < 336, tap, -64), jnp.where(kind == 2, 16 + (j & 7), j)


def pack_stats(first, second):
    return jnp.concatenate([first[:, :128], first[:, 128:], second[:, :128], second[:, 128:], jnp.zeros((4, 128), F32)], axis=0)


def kernel(
    clip_in, rows_in, cols_in, start_in, feats_in, feats4, grads_in, grads4, weight_in, gamma_in, beta_in, bias_in,
    conv_out, in_grad, wg_out,
    halo_x, halo_g, plane_st, z_st, plane_bk, z_bk,
    wsh, sel_s, pair_w, zbuf, wall, hsh, gsh, gt, prod, s0buf, qsum, s1a, s1b, rsum, s2buf, s3own, s3src, s3buf, s4src,
    acc_e, acc_o, acc_h, normed_s, dfac_s, stat_s,
    clip, rows, cols, start, feats, grads, weight, gamma, beta, bias,
    sem_in, sem_halo, sem_st, sem_bk, sem_w, sem_rs,
):
    d, t = lax.axis_index("dp"), lax.axis_index("tile")
    y, xh = d // 2, d % 2
    z, xl, core = t // 4, (t // 2) % 2, t % 2
    x = xh * 2 + xl
    other = 1 - core

    def device(px, py, pz, pc):
        return (py * 2 + px // 2, pz * 4 + (px % 2) * 2 + pc)

    def first_peer(j):
        return device((x + j * core) % 4, (y + j * other) % 4, z, core)

    def second_peer(j):
        return device((x + j * other) % 4, (y + j * core) % 4, z, core)

    def z_peer(j):
        return device(x, y, (z + j) % 8, core)

    own_f = y * other + x * core
    own_s = x * other + y * core
    sibling = device(x, y, z, other)
    beside = device(xh * 2 + 1 - xl, y, z, core)
    diagonal = device(xh * 2 + 1 - xl, y, z, other)
    above_t, below_t = (t + 31) % 32, (t + 1) % 32

    def copy(src, dst, sems, k, target):
        return pltpu.make_async_remote_copy(
            src_ref=src, dst_ref=dst, send_sem=sems.at[0, k], recv_sem=sems.at[1, k],
            device_id=target, device_id_type=MESH,
        )

    barrier = pltpu.get_barrier_semaphore()
    peers = [sibling, diagonal, (d, above_t), (d, below_t)]
    peers += [z_peer(j) for j in range(1, 8)]
    peers += [first_peer(j) for j in (1, 2, 3)] + [second_peer(j) for j in (1, 2, 3)]
    for peer in peers:
        pl.semaphore_signal(barrier, inc=1, device_id=peer, device_id_type=MESH)

    fetches = [
        pltpu.make_async_copy(src, dst, sem_in.at[k])
        for k, (src, dst) in enumerate((
            (clip_in, clip), (rows_in, rows), (cols_in, cols), (start_in, start), (feats_in, feats), (grads_in, grads),
            (weight_in, weight), (gamma_in, gamma), (beta_in, beta), (bias_in, bias),
        ))
    ]
    for c in fetches:
        c.start()
    for c in fetches:
        c.wait()

    own = clip[0, t]
    first = start[0, own]
    ncols = cols[0, own]
    nrows = rows[0, t]
    weights = [jnp.where(clip[0, k] == own, 1, 0) for k in range(32)]
    clip_rows = functools.reduce(lambda a, b: a + b, [weights[k] * rows[0, k] for k in range(32)])
    scale = 1.0 / (jnp.full((1, 128), (4 - first) * ncols * clip_rows * 6, I32).astype(F32))
    keep_above = jnp.where((t > 0) & (clip[0, above_t] == own) & (rows[0, above_t] > 7), 1, 0)
    keep_below = jnp.where((t < 31) & (clip[0, below_t] == own), 1, 0)

    n = iota((256, 128), 0)
    vmask = one_hot(((n >> 6) >= first) & (((n >> 3) & 7) < nrows) & ((n & 7) < ncols), F32)
    n = iota((64, 128), 0)
    keep = jnp.where(n < 32, keep_above, keep_below)
    rmask = one_hot((((n >> 3) & 3) >= first) & ((n & 7) < ncols) & (keep == 1), F32)
    vmask2, rmask2 = twice(vmask), twice(rmask)

    spread_in = one_hot(iota((192, 256), 0) == in_channel(iota((192, 256), 1)), BF16)
    masked = dot(feats[...], spread_in) * vmask2
    stats = pack_stats(jnp.sum(masked, axis=0, keepdims=True), jnp.sum(masked * masked, axis=0, keepdims=True))
    plane_st[xl * 2 + core] = stats

    tap_lane, out_lane = place(iota((27, 384), 1))
    for h in range(2):
        sel_s[h] = one_hot(tap_lane + 14 * h == iota((27, 384), 0), BF16)
    out_mask = one_hot(place(iota((24, 384), 1))[1] == iota((24, 384), 0), F32)
    flat = weight[...].astype(F32).reshape(144, 27).astype(BF16)
    for h in range(2):
        spread = dot(flat, sel_s[h]).reshape(6, 24, 384) * out_mask[None]
        wsh[h] = jnp.concatenate([jnp.sum(spread, axis=1), jnp.zeros((2, 384), F32)], axis=0)
    pair_w[core] = wsh[core]

    pl.semaphore_wait(barrier, len(peers))

    pair_copy = copy(wsh.at[other], pair_w.at[core], sem_w, 0, sibling)
    pair_copy.start()

    def plane_send(buf, sems):
        q = xl * 2 + core
        out = [copy(buf.at[q], buf.at[q], sems, k, peer) for k, peer in enumerate((sibling, beside, diagonal))]
        for c in out:
            c.start()
        return out

    def z_send(plane, buf, sems, copies):
        for c in copies:
            c.wait_recv()
        buf[z] = jnp.concatenate([plane[q][:4] for q in range(4)], axis=0)
        out = [copy(buf.at[z], buf.at[z], sems, 2 + j, z_peer(j)) for j in range(1, 8)]
        for c in out:
            c.start()
        return out

    def clip_sums(buf, copies):
        for c in copies:
            c.wait_recv()
        row = iota((16, 128), 0) >> 2
        total = jnp.zeros((16, 128), F32)
        for k in range(8):
            w = [weights[4 * k + q] for q in range(4)]
            wrow = jnp.where(row == 0, w[0], jnp.where(row == 1, w[1], jnp.where(row == 2, w[2], w[3])))
            total = total + jnp.where(wrow == 1, buf[k], 0.0)
        total = group_sum(total[0:4] + total[4:8] + total[8:12] + total[12:16])
        halves = total * scale
        return (
            jnp.concatenate([halves[0:1], halves[1:2]], axis=1),
            jnp.concatenate([halves[2:3], halves[3:4]], axis=1),
        )

    st1 = plane_send(plane_st, sem_st)
    halos = [
        copy(feats4.at[:, 7], halo_x.at[0], sem_halo, 0, (d, below_t)),
        copy(feats4.at[:, 0], halo_x.at[1], sem_halo, 1, (d, above_t)),
        copy(grads4.at[:, 7], halo_g.at[0], sem_halo, 2, (d, below_t)),
        copy(grads4.at[:, 0], halo_g.at[1], sem_halo, 3, (d, above_t)),
    ]
    for c in halos:
        c.start()

    pair_copy.wait_recv()
    zbuf[z] = pair_w[...].reshape(16, 384).astype(BF16)
    zw = [copy(zbuf.at[z], zbuf.at[z], sem_w, j, z_peer(j)) for j in range(1, 8)]
    for c in zw:
        c.start()
    st2 = z_send(plane_st, z_st, sem_st, st1)

    hsh[:, 0:128, :] = jnp.zeros((9, 128, 256), BF16)
    gsh[:, 256:384, :] = jnp.zeros((9, 128, 384), BF16)
    spread_out = one_hot(iota((192, 384), 0) == out_channel(iota((192, 384), 1)), BF16)
    ge = dot(grads[...], spread_out) * jnp.concatenate([vmask, vmask, vmask], axis=1)
    get = ge.T.astype(BF16)
    gt[0:256] = get[0:256]
    gt[256:384] = get[0:128]
    gt[384:512] = get[256:384]
    halos[2].wait_recv()
    halos[3].wait_recv()
    gr = dot(halo_g[...].astype(F32).reshape(64, 192).astype(BF16), spread_out)
    put_shifts(extend(ge, gr * jnp.concatenate([rmask, rmask, rmask], axis=1)), gsh, 0)

    for c in zw:
        c.wait_recv()
    wall[core, own_f, own_s] = zbuf[...].astype(F32).reshape(128, 384).T[0:336].astype(BF16)
    w2 = [copy(wall.at[core, own_f, own_s], wall.at[core, own_f, own_s], sem_w, 7 + j, second_peer(j)) for j in (1, 2, 3)]
    for c in w2:
        c.start()

    mean, square = clip_sums(z_st, st2)
    inv_std = lax.rsqrt(square - mean * mean + EPSILON)
    spread_f32 = spread_in.astype(F32)
    gamma_l = exact_dot(gamma[...], spread_f32)
    beta_l = exact_dot(beta[...], spread_f32)
    normed = (masked - mean) * inv_std
    act = normed * gamma_l + beta_l
    sig = 1.0 / (1.0 + jnp.exp(-act))
    normed_s[...] = normed
    dfac_s[...] = vmask2 * sig * (1.0 + act * (1.0 - sig)) * gamma_l
    halos[0].wait_recv()
    halos[1].wait_recv()
    rim = dot(halo_x[...].astype(F32).reshape(64, 192).astype(BF16), spread_in)
    rim_act = (rim * rmask2 - mean) * inv_std * gamma_l + beta_l
    rim_hidden = rim_act / (1.0 + jnp.exp(-rim_act)) * rmask2
    put_shifts(extend(act * sig * vmask2, rim_hidden), hsh, 128)

    def tap_of(tap):
        tap = tap - tap // 27
        return tap // 9, tap % 9

    def hidden_tap(tap):
        a, be = tap_of(tap)
        return hsh[be, pl.ds(pl.multiple_of(a * 64, 64), 256), :]

    def piece(h, dd, ll):
        py, px = dd // 2, (dd % 2) * 2 + ll
        return py * (1 - h) + px * h, px * (1 - h) + py * h

    def strip(p, kind):
        return pl.ds(p * 48 + kind * 16, 16)

    def product(h, low, high, final):
        for p in range(low, high):
            ra = dot(gt[0:256], hidden_tap(h * 14 + 2 * p))
            rb = dot(gt[256:512], hidden_tap(h * 14 + 2 * p + 1))
            for kind, value in enumerate((ra[0:128], rb[0:128], ra[128:256] + rb[128:256])):
                for dd in range(8):
                    for ll in range(2):
                        f, s = piece(h, dd, ll)
                        tile = value[dd * 16 : dd * 16 + 16, ll * 128 : ll * 128 + 128]
                        if final:
                            qsum[f, s, strip(p, kind), :] = (tile + s0buf[f, s, strip(p, kind), :].astype(F32)).astype(BF16)
                        else:
                            prod[f, s, strip(p, kind), :] = tile.astype(BF16)

    chunks = ((0, 4), (4, 7))
    spans = [pl.ds(48 * low, 48 * (high - low)) for low, high in chunks]
    every = pl.ds(0, 4)
    s0 = []
    for k, (low, high) in enumerate(chunks):
        product(other, low, high, False)
        s0.append(copy(prod.at[every, every, spans[k]], s0buf.at[every, every, spans[k]], sem_rs, k, sibling))
        s0[k].start()

    next_f, far_f, last_f = (own_f + 1) % 4, (own_f + 2) % 4, (own_f + 3) % 4
    left, right = pl.ds(0, 2), pl.ds(2, 2)

    def wcopy(f, part, k, target):
        return copy(wall.at[core, f, part], wall.at[core, f, part], sem_w, k, target)

    for c in w2:
        c.wait_recv()
    w3 = [
        wcopy(own_f, left, 11, first_peer(1)), wcopy(own_f, right, 12, first_peer(3)),
        wcopy(own_f, right, 13, first_peer(1)), wcopy(own_f, left, 14, first_peer(3)),
    ]
    for c in w3:
        c.start()
    w4 = [wcopy(own_f, every, 17, sibling)]
    w4[0].start()

    s1 = []
    for k, (low, high) in enumerate(chunks):
        s0[k].wait_recv()
        product(core, low, high, True)
        s1.append([
            copy(qsum.at[far_f, left, spans[k]], s1a.at[0, left, spans[k]], sem_rs, 2 + 2 * k, first_peer(1)),
            copy(qsum.at[far_f, right, spans[k]], s1a.at[1, left, spans[k]], sem_rs, 3 + 2 * k, first_peer(3)),
        ])
        for c in s1[k]:
            c.start()

    w3[0].wait_recv()
    w5 = [wcopy(last_f, left, 15, first_peer(1))]
    w5[0].start()
    w3[1].wait_recv()
    w5.append(wcopy(next_f, right, 16, first_peer(3)))
    w5[1].start()

    s1n = []
    for k in range(2):
        for c in s1[k]:
            c.wait_recv()
        for s in range(2):
            qsum[next_f, s, spans[k]] = (qsum[next_f, s, spans[k]].astype(F32) + s1a[0, s, spans[k]].astype(F32)).astype(BF16)
            qsum[last_f, 2 + s, spans[k]] = (qsum[last_f, 2 + s, spans[k]].astype(F32) + s1a[1, s, spans[k]].astype(F32)).astype(BF16)
        s1n.append([
            copy(qsum.at[next_f, every, spans[k]], s1b.at[0, every, spans[k]], sem_rs, 6 + 2 * k, first_peer(1)),
            copy(qsum.at[last_f, every, spans[k]], s1b.at[1, every, spans[k]], sem_rs, 7 + 2 * k, first_peer(3)),
        ])
        for c in s1n[k]:
            c.start()

    w3[2].wait_recv()
    w4.append(wcopy(last_f, every, 18, sibling))
    w4[1].start()
    w3[3].wait_recv()
    w4.append(wcopy(next_f, every, 19, sibling))
    w4[2].start()
    for c in w5:
        c.wait_recv()
    w4.append(wcopy(far_f, every, 20, sibling))
    w4[3].start()

    def tap_weight(h, p, kind):
        lanes = []
        for ll in range(2):
            parts = []
            for dd in range(8):
                f, s = piece(h, dd, ll)
                parts.append(wall[h, f, s, strip(p, kind), :])
            lanes.append(jnp.concatenate(parts, axis=0))
        return jnp.concatenate(lanes, axis=1)

    def tap_weights(h, p):
        shared = tap_weight(h, p, 2)
        return [jnp.concatenate([tap_weight(h, p, kind), shared], axis=0) for kind in range(2)]

    def grad_tap(tap, tail):
        a, be = tap_of(tap)
        rows_ = pl.ds(pl.multiple_of((2 - a) * 64, 64), 256)
        return jnp.concatenate([gsh[8 - be, rows_, 0:128], gsh[8 - be, rows_, 128 * tail : 128 * tail + 128]], axis=1)

    def hidden_half(h, fresh):
        for p in range(7):
            tap = h * 14 + 2 * p
            wa, wb = tap_weights(h, p)
            lhs = jnp.concatenate([grad_tap(tap, 1), grad_tap(tap + 1, 2)], axis=1)
            value = dot(lhs, jnp.concatenate([wa, wb], axis=0))
            if fresh and p == 0:
                acc_h[...] = value
            else:
                acc_h[...] += value

    def conv_half(h, fresh):
        for group in ((0, 1), (2, 3), (4, 5), (6,)):
            both = [tap_weights(h, p) for p in group]
            for odd, acc in enumerate((acc_e, acc_o)):
                lhs = jnp.concatenate([hidden_tap(h * 14 + 2 * p + odd) for p in group], axis=1)
                rhs = jnp.concatenate([w[odd] for w in both], axis=1)
                value = lax.dot_general(lhs, rhs, NT_DIMS, preferred_element_type=F32)
                if fresh and group[0] == 0:
                    acc[...] = value
                else:
                    acc[...] += value

    hidden_half(core, True)

    for pair in s1n:
        for c in pair:
            c.wait_recv()

    def first_total(s):
        return qsum[own_f, s].astype(F32) + s1b[0, s].astype(F32) + s1b[1, s].astype(F32)

    def add_first(s, carry):
        rsum[s] = first_total(s).astype(BF16)
        return carry

    lax.fori_loop(0, 4, add_first, 0)
    s2 = [copy(rsum.at[(own_s + j) % 4], s2buf.at[j - 1], sem_rs, 9 + j, second_peer(j)) for j in (1, 2, 3)]
    for c in s2:
        c.start()
    for c in w4:
        c.wait_recv()
    hidden_half(other, False)

    dn = acc_h[...] * dfac_s[...]
    back = pack_stats(jnp.sum(dn, axis=0, keepdims=True), jnp.sum(dn * normed_s[...], axis=0, keepdims=True))
    acc_h[...] = dn
    plane_bk[xl * 2 + core] = back
    bk1 = plane_send(plane_bk, sem_bk)

    for c in s2:
        c.wait_recv()
    total = first_total(own_s)
    for j in range(3):
        total = total + s2buf[j].astype(F32)
    total = jnp.concatenate([total, jnp.zeros((48, 128), F32)], axis=0).T.reshape(8, 16, 384)
    s3own[...] = total
    s3src[...] = total.astype(BF16)
    s3 = [copy(s3src.at[(z + j) % 8], s3buf.at[j - 1], sem_rs, 12 + j, z_peer(j)) for j in range(1, 8)]
    for c in s3:
        c.start()
    bk2 = z_send(plane_bk, z_bk, sem_bk, bk1)

    conv_half(core, True)
    conv_half(other, False)

    lane256 = iota((256, 192), 0)
    pack_out = one_hot(jnp.where(lane256 < 128, out_channel(lane256), jnp.where((lane256 & 15) < 8, out_channel(lane256), -1)) == iota((256, 192), 1), BF16)
    bias_l = exact_dot(bias[...], spread_out[:, 0:256].astype(F32))
    tail_odd = pltpu.roll(acc_o[:, 128:256], 120, 1)
    conv = jnp.concatenate([acc_e[:, 0:128] + acc_o[:, 0:128], acc_e[:, 128:256] + tail_odd], axis=1)
    conv = ((conv + bias_l) * vmask2).astype(BF16)
    conv_out[...] = dot(conv, pack_out).astype(BF16)

    sum_one, sum_two = clip_sums(z_bk, bk2)
    pack_in = one_hot(in_channel(iota((256, 192), 0)) == iota((256, 192), 1), BF16)
    grad_x = inv_std * (acc_h[...] - sum_one - normed_s[...] * sum_two) * vmask2
    in_grad[...] = dot(grad_x.astype(BF16), pack_in).astype(BF16)

    for c in s3:
        c.wait_recv()
    total = s3own[z]
    for j in range(7):
        total = total + s3buf[j].astype(F32)
    s4src[...] = total.reshape(2, 8, 384)
    s4 = copy(s4src.at[other], stat_s, sem_rs, 20, sibling)
    s4.start()

    def unpack(value, h):
        flat = (value[0:6].reshape(6, 1, 384) * out_mask[None]).reshape(144, 384)
        high = flat.astype(BF16)
        low = (flat - high.astype(F32)).astype(BF16)
        return sum(lax.dot_general(v, sel_s[h], NT_DIMS, preferred_element_type=F32) for v in (high, low))

    own_part = unpack(s4src[core], core)
    s4.wait_recv()
    wg_out[...] = (own_part + unpack(stat_s[...], other)).reshape(6, 24, 27)
    for c in [pair_copy, s4] + zw + w2 + w3 + w4 + w5 + s0 + s1[0] + s1[1] + s1n[0] + s1n[1] + s2 + s3 + st1 + st2 + bk1 + bk2 + halos:
        c.wait_send()


def emit(conv, grad, wg, conv_out, grad_out, wg_out):
    conv_out[...] = conv[...]
    grad_out[...] = grad[...]
    wg_out[...] = wg[...]


def on_device(features, out_grad, weight, bias, gamma, beta, tile_clip, tile_rows, clip_cols, clip_start):
    dma = pltpu.SemaphoreType.DMA
    vmem, anywhere = pl.BlockSpec(memory_space=pltpu.VMEM), pl.BlockSpec(memory_space=pl.ANY)
    conv_out, in_grad, wg = pl.pallas_call(
        kernel,
        out_shape=(
            jax.ShapeDtypeStruct((256, 192), BF16),
            jax.ShapeDtypeStruct((256, 192), BF16),
            jax.ShapeDtypeStruct((6, 24, 27), F32),
        ),
        in_specs=[anywhere] * 12,
        out_specs=[vmem] * 3,
        scratch_shapes=[
            pltpu.VMEM((2, 4, 8, 192), BF16),
            pltpu.VMEM((2, 4, 8, 192), BF16),
            pltpu.VMEM((4, 8, 128), F32),
            pltpu.VMEM((8, 16, 128), F32),
            pltpu.VMEM((4, 8, 128), F32),
            pltpu.VMEM((8, 16, 128), F32),
            pltpu.VMEM((2, 8, 384), F32),
            pltpu.VMEM((2, 27, 384), BF16),
            pltpu.VMEM((2, 8, 384), F32),
            pltpu.VMEM((8, 16, 384), BF16),
            pltpu.VMEM((2, 4, 4, 336, 128), BF16),
            pltpu.VMEM((9, 384, 256), BF16),
            pltpu.VMEM((9, 384, 384), BF16),
            pltpu.VMEM((512, 256), BF16),
            pltpu.VMEM((4, 4, 336, 128), BF16),
            pltpu.VMEM((4, 4, 336, 128), BF16),
            pltpu.VMEM((4, 4, 336, 128), BF16),
            pltpu.VMEM((2, 2, 336, 128), BF16),
            pltpu.VMEM((2, 4, 336, 128), BF16),
            pltpu.VMEM((4, 336, 128), BF16),
            pltpu.VMEM((3, 336, 128), BF16),
            pltpu.VMEM((8, 16, 384), F32),
            pltpu.VMEM((8, 16, 384), BF16),
            pltpu.VMEM((7, 16, 384), BF16),
            pltpu.VMEM((2, 8, 384), F32),
            pltpu.VMEM((256, 256), F32),
            pltpu.VMEM((256, 256), F32),
            pltpu.VMEM((256, 256), F32),
            pltpu.VMEM((256, 256), F32),
            pltpu.VMEM((256, 256), F32),
            pltpu.VMEM((8, 384), F32),
            pltpu.SMEM((1, 32), I32),
            pltpu.SMEM((1, 32), I32),
            pltpu.SMEM((1, 32), I32),
            pltpu.SMEM((1, 32), I32),
            pltpu.VMEM((256, 192), BF16),
            pltpu.VMEM((256, 192), BF16),
            pltpu.VMEM((6, 24, 27), BF16),
            pltpu.VMEM((1, 192), F32),
            pltpu.VMEM((1, 192), F32),
            pltpu.VMEM((1, 192), F32),
            dma((10,)),
            dma((2, 4)),
            dma((2, 10)),
            dma((2, 10)),
            dma((2, 21)),
            dma((2, 21)),
        ],
        compiler_params=pltpu.CompilerParams(collective_id=0, has_side_effects=True, vmem_limit_bytes=56 * 1024 * 1024),
    )(
        tile_clip, tile_rows, clip_cols, clip_start,
        features.reshape(256, 192), features.reshape(4, 8, 8, 192),
        out_grad.reshape(256, 192), out_grad.reshape(4, 8, 8, 192),
        weight.transpose(0, 2, 1), gamma.reshape(1, 192), beta.reshape(1, 192), bias.reshape(1, 192),
    )
    conv_out, in_grad, wg = pl.pallas_call(
        emit,
        out_shape=tuple(jax.ShapeDtypeStruct(v.shape, v.dtype) for v in (conv_out, in_grad, wg)),
        in_specs=[vmem] * 3,
        out_specs=[vmem] * 3,
    )(conv_out, in_grad, wg)
    return (conv_out.reshape(features.shape), in_grad.reshape(features.shape), wg.transpose(0, 2, 1))


def solution(mesh):
    in_specs = (
        P("dp", None, "tile", None, None),
        P("dp", None, "tile", None, None),
        P("tile", None, "dp"),
        P(),
        P(),
        P(),
        P("dp", None),
        P("dp", None),
        P("dp", None),
        P("dp", None),
    )
    out_specs = (
        P("dp", None, "tile", None, None),
        P("dp", None, "tile", None, None),
        P("tile", None, "dp"),
    )
    return jax.shard_map(on_device, mesh=mesh, in_specs=in_specs, out_specs=out_specs, check_vma=False)
```

```python
import functools

import jax
import jax.numpy as jnp
from jax import lax
from jax.experimental import pallas as pl
from jax.experimental.pallas import tpu as pltpu
from jax.sharding import PartitionSpec as P


MESH = pl.DeviceIdType.MESH
F32, BF16, I32 = jnp.float32, jnp.bfloat16, jnp.int32
EPSILON = 1e-05
NT_DIMS = (((1,), (1,)), ((), ()))


def iota(shape, dim):
    return lax.broadcasted_iota(I32, shape, dim)


def in_channel(lane):
    group, r = (((lane >> 4) & 7) * 4 + (lane >> 7) * 2 + ((lane >> 3) & 1)), lane & 7
    return jnp.where(r < 6, group * 6 + r, -1)


def out_channel(lane):
    kind, m = lane >> 7, lane & 127
    d, j = m >> 4, m & 15
    tail = jnp.where(kind == 1, jnp.where(j < 8, d * 24 + 16 + j, -1), jnp.where(j >= 8, d * 24 + 8 + j, -1))
    return jnp.where(kind == 0, d * 24 + j, tail)


def one_hot(equal, dtype):
    return jnp.where(equal, 1.0, 0.0).astype(dtype)


def dot(a, b):
    return jnp.dot(a, b, preferred_element_type=F32)


def exact_dot(a, b):
    return jnp.dot(a, b, preferred_element_type=F32, precision=lax.Precision.HIGHEST)


def twice(mask):
    return jnp.concatenate([mask, mask], axis=1)


def group_sum(s):
    lane = iota(s.shape, 1)
    for shift in (1, 2, 4):
        s = s + jnp.where((lane & shift) != 0, pltpu.roll(s, shift, 1), pltpu.roll(s, 128 - shift, 1))
    return s


def extend(centre, rims):
    lanes = centre.shape[1]
    above = rims[:32].reshape(4, 1, 8, lanes)
    below = rims[32:].reshape(4, 1, 8, lanes)
    return jnp.concatenate([above, centre.reshape(4, 8, 8, lanes), below], axis=1).reshape(320, lanes)


def put_shifts(ext, dst, first_row):
    lanes = ext.shape[1]
    col = iota(ext.shape, 0) & 7
    for e in range(3):
        if e == 0:
            moved = jnp.where(col == 0, 0.0, pltpu.roll(ext, 1, 0))
        elif e == 1:
            moved = ext
        else:
            moved = jnp.where(col == 7, 0.0, pltpu.roll(ext, 319, 0))
        moved = moved.reshape(4, 10, 8, lanes)
        for b in range(3):
            dst[3 * b + e, first_row : first_row + 256, :] = moved[:, b : b + 8].reshape(256, lanes).astype(BF16)


def place(lane):
    u, j = lane >> 4, lane & 15
    p = (u * 171) >> 9
    kind = u - 3 * p
    tap = 2 * p + jnp.where(kind == 2, j >> 3, kind)
    return jnp.where(lane < 336, tap, -64), jnp.where(kind == 2, 16 + (j & 7), j)


def pack_stats(first, second):
    return jnp.concatenate([first[:, :128], first[:, 128:], second[:, :128], second[:, 128:]], axis=0)


def kernel(
    clip_in, rows_in, cols_in, start_in, feats_in, feats4, grads_in, grads4, weight_in, gamma_in, beta_in, bias_in,
    conv_out, in_grad, wg_out,
    halo_x, halo_g, all_st, all_bk,
    wsh, sel_s, zbuf, wall, hsh, gsh, gt, prod, s0buf, qsum, s1a, s1b, rsum, s2buf, s3own, s3src, s3buf,
    acc_e, acc_o, acc_h, normed_s, dfac_s,
    clip, rows, cols, start, feats, grads, weight, gamma, beta, bias,
    sem_in, sem_halo, sem_st, sem_bk, sem_w, sem_rs,
):
    d, t = lax.axis_index("dp"), lax.axis_index("tile")
    y, xh = d // 2, d % 2
    z, xl, core = t // 4, (t // 2) % 2, t % 2
    x = xh * 2 + xl
    other = 1 - core

    def device(px, py, pz, pc):
        return (py * 2 + px // 2, pz * 4 + (px % 2) * 2 + pc)

    def first_peer(j):
        return device((x + j * core) % 4, (y + j * other) % 4, z, core)

    def second_peer(j):
        return device((x + j * other) % 4, (y + j * core) % 4, z, core)

    def z_peer(j):
        return device(x, y, (z + j) % 8, core)

    own_f = y * other + x * core
    own_s = x * other + y * core
    sibling = device(x, y, z, other)
    above_t, below_t = (t + 31) % 32, (t + 1) % 32

    def copy(src, dst, sems, k, target):
        return pltpu.make_async_remote_copy(
            src_ref=src, dst_ref=dst, send_sem=sems.at[0, k], recv_sem=sems.at[1, k],
            device_id=target, device_id_type=MESH,
        )

    barrier = pltpu.get_barrier_semaphore()
    peers = [(d, (t + k) % 32) for k in range(1, 32)]
    peers += [first_peer(j) for j in (1, 2, 3)] + [second_peer(j) for j in (1, 2, 3)]
    for peer in peers:
        pl.semaphore_signal(barrier, inc=1, device_id=peer, device_id_type=MESH)

    fetches = [
        pltpu.make_async_copy(src, dst, sem_in.at[k])
        for k, (src, dst) in enumerate((
            (clip_in, clip), (rows_in, rows), (cols_in, cols), (start_in, start), (feats_in, feats), (grads_in, grads),
            (weight_in, weight), (gamma_in, gamma), (beta_in, beta), (bias_in, bias),
        ))
    ]
    for c in fetches:
        c.start()
    for c in fetches:
        c.wait()

    own = clip[0, t]
    first = start[0, own]
    ncols = cols[0, own]
    nrows = rows[0, t]
    weights = [jnp.where(clip[0, k] == own, 1, 0) for k in range(32)]
    clip_rows = functools.reduce(lambda a, b: a + b, [weights[k] * rows[0, k] for k in range(32)])
    scale = 1.0 / (jnp.full((1, 128), (4 - first) * ncols * clip_rows * 6, I32).astype(F32))
    keep_above = jnp.where((t > 0) & (clip[0, above_t] == own) & (rows[0, above_t] > 7), 1, 0)
    keep_below = jnp.where((t < 31) & (clip[0, below_t] == own), 1, 0)

    n = iota((256, 128), 0)
    vmask = one_hot(((n >> 6) >= first) & (((n >> 3) & 7) < nrows) & ((n & 7) < ncols), F32)
    n = iota((64, 128), 0)
    keep = jnp.where(n < 32, keep_above, keep_below)
    rmask = one_hot((((n >> 3) & 3) >= first) & ((n & 7) < ncols) & (keep == 1), F32)
    vmask2, rmask2 = twice(vmask), twice(rmask)

    spread_in = one_hot(iota((192, 256), 0) == in_channel(iota((192, 256), 1)), BF16)
    masked = dot(feats[...], spread_in) * vmask2
    stats = pack_stats(jnp.sum(masked, axis=0, keepdims=True), jnp.sum(masked * masked, axis=0, keepdims=True))
    all_st[t] = stats

    tap_lane, out_lane = place(iota((27, 384), 1))
    for h in range(2):
        sel_s[h] = one_hot(tap_lane + 14 * h == iota((27, 384), 0), BF16)
    out_mask = one_hot(place(iota((24, 384), 1))[1] == iota((24, 384), 0), F32)
    flat = weight[...].astype(F32).reshape(144, 27).astype(BF16)
    for h in range(2):
        spread = dot(flat, sel_s[h]).reshape(6, 24, 384) * out_mask[None]
        wsh[h] = jnp.concatenate([jnp.sum(spread, axis=1), jnp.zeros((2, 384), F32)], axis=0).astype(BF16)
    zbuf[z, core] = wsh[core]

    pl.semaphore_wait(barrier, len(peers))

    def to_all(buf, sems):
        out = [copy(buf.at[t], buf.at[t], sems, k - 1, (d, (t + k) % 32)) for k in range(1, 32)]
        for c in out:
            c.start()
        return out

    zw = [copy(wsh.at[core], zbuf.at[z, core], sem_w, j - 1, z_peer(j)) for j in range(1, 8)]
    zw += [copy(wsh.at[other], zbuf.at[z, core], sem_w, 7 + j, device(x, y, (z + j) % 8, other)) for j in range(8)]
    for c in zw:
        c.start()

    st = to_all(all_st, sem_st)

    def clip_sums(buf, copies):
        for c in copies:
            c.wait_recv()
        parts = [jnp.where(weights[k] == 1, buf[k], 0.0) for k in range(32)]
        while len(parts) > 1:
            parts = [a + b for a, b in zip(parts[::2], parts[1::2])]
        total = group_sum(parts[0])
        halves = total * scale
        return (
            jnp.concatenate([halves[0:1], halves[1:2]], axis=1),
            jnp.concatenate([halves[2:3], halves[3:4]], axis=1),
        )

    halos = [
        copy(feats4.at[:, 7], halo_x.at[0], sem_halo, 0, (d, below_t)),
        copy(feats4.at[:, 0], halo_x.at[1], sem_halo, 1, (d, above_t)),
        copy(grads4.at[:, 7], halo_g.at[0], sem_halo, 2, (d, below_t)),
        copy(grads4.at[:, 0], halo_g.at[1], sem_halo, 3, (d, above_t)),
    ]
    for c in halos:
        c.start()

    hsh[:, 0:128, :] = jnp.zeros((9, 128, 256), BF16)
    gsh[:, 256:384, :] = jnp.zeros((9, 128, 384), BF16)
    spread_out = one_hot(iota((192, 384), 0) == out_channel(iota((192, 384), 1)), BF16)
    ge = dot(grads[...], spread_out) * jnp.concatenate([vmask, vmask, vmask], axis=1)
    get = ge.T.astype(BF16)
    gt[0:256] = get[0:256]
    gt[256:384] = get[0:128]
    gt[384:512] = get[256:384]
    halos[2].wait_recv()
    halos[3].wait_recv()
    gr = dot(halo_g[...].astype(F32).reshape(64, 192).astype(BF16), spread_out)
    put_shifts(extend(ge, gr * jnp.concatenate([rmask, rmask, rmask], axis=1)), gsh, 0)

    for c in zw:
        c.wait_recv()
    wall[core, own_f, own_s] = zbuf[...].astype(F32).reshape(128, 384).T[0:336].astype(BF16)
    w2 = [copy(wall.at[core, own_f, own_s], wall.at[core, own_f, own_s], sem_w, 14 + j, second_peer(j)) for j in (1, 2, 3)]
    for c in w2:
        c.start()

    mean, square = clip_sums(all_st, st)
    inv_std = lax.rsqrt(square - mean * mean + EPSILON)
    spread_f32 = spread_in.astype(F32)
    gamma_l = exact_dot(gamma[...], spread_f32)
    beta_l = exact_dot(beta[...], spread_f32)
    normed = (masked - mean) * inv_std
    act = normed * gamma_l + beta_l
    sig = 1.0 / (1.0 + jnp.exp(-act))
    normed_s[...] = normed
    dfac_s[...] = vmask2 * sig * (1.0 + act * (1.0 - sig)) * gamma_l
    halos[0].wait_recv()
    halos[1].wait_recv()
    rim = dot(halo_x[...].astype(F32).reshape(64, 192).astype(BF16), spread_in)
    rim_act = (rim * rmask2 - mean) * inv_std * gamma_l + beta_l
    rim_hidden = rim_act / (1.0 + jnp.exp(-rim_act)) * rmask2
    put_shifts(extend(act * sig * vmask2, rim_hidden), hsh, 128)

    def tap_of(tap):
        tap = tap - tap // 27
        return tap // 9, tap % 9

    def hidden_tap(tap):
        a, be = tap_of(tap)
        return hsh[be, pl.ds(pl.multiple_of(a * 64, 64), 256), :]

    def piece(h, dd, ll):
        py, px = dd // 2, (dd % 2) * 2 + ll
        return py * (1 - h) + px * h, px * (1 - h) + py * h

    def strip(p, kind):
        return pl.ds(p * 48 + kind * 16, 16)

    def product(h, low, high, final):
        for p in range(low, high):
            ra = dot(gt[0:256], hidden_tap(h * 14 + 2 * p))
            rb = dot(gt[256:512], hidden_tap(h * 14 + 2 * p + 1))
            for kind, value in enumerate((ra[0:128], rb[0:128], ra[128:256] + rb[128:256])):
                for dd in range(8):
                    for ll in range(2):
                        f, s = piece(h, dd, ll)
                        tile = value[dd * 16 : dd * 16 + 16, ll * 128 : ll * 128 + 128]
                        if final:
                            qsum[f, s, strip(p, kind), :] = (tile + s0buf[f, s, strip(p, kind), :].astype(F32)).astype(BF16)
                        else:
                            prod[f, s, strip(p, kind), :] = tile.astype(BF16)

    chunks = ((0, 4), (4, 7))
    spans = [pl.ds(48 * low, 48 * (high - low)) for low, high in chunks]
    every = pl.ds(0, 4)
    s0 = []
    for k, (low, high) in enumerate(chunks):
        product(other, low, high, False)
        s0.append(copy(prod.at[every, every, spans[k]], s0buf.at[every, every, spans[k]], sem_rs, k, sibling))
        s0[k].start()

    next_f, far_f, last_f = (own_f + 1) % 4, (own_f + 2) % 4, (own_f + 3) % 4
    left, right = pl.ds(0, 2), pl.ds(2, 2)

    def wcopy(f, part, k, target):
        return copy(wall.at[core, f, part], wall.at[core, f, part], sem_w, k, target)

    for c in w2:
        c.wait_recv()
    w3 = [
        wcopy(own_f, left, 18, first_peer(1)), wcopy(own_f, right, 19, first_peer(3)),
        wcopy(own_f, right, 20, first_peer(1)), wcopy(own_f, left, 21, first_peer(3)),
    ]
    for c in w3:
        c.start()
    w4 = [wcopy(own_f, every, 24, sibling)]
    w4[0].start()

    s1 = []
    for k, (low, high) in enumerate(chunks):
        s0[k].wait_recv()
        product(core, low, high, True)
        s1.append([
            copy(qsum.at[far_f, left, spans[k]], s1a.at[0, left, spans[k]], sem_rs, 2 + 2 * k, first_peer(1)),
            copy(qsum.at[far_f, right, spans[k]], s1a.at[1, left, spans[k]], sem_rs, 3 + 2 * k, first_peer(3)),
        ])
        for c in s1[k]:
            c.start()

    w3[0].wait_recv()
    w5 = [wcopy(last_f, left, 22, first_peer(1))]
    w5[0].start()
    w3[1].wait_recv()
    w5.append(wcopy(next_f, right, 23, first_peer(3)))
    w5[1].start()

    s1n = []
    for k in range(2):
        for c in s1[k]:
            c.wait_recv()
        for s in range(2):
            qsum[next_f, s, spans[k]] = (qsum[next_f, s, spans[k]].astype(F32) + s1a[0, s, spans[k]].astype(F32)).astype(BF16)
            qsum[last_f, 2 + s, spans[k]] = (qsum[last_f, 2 + s, spans[k]].astype(F32) + s1a[1, s, spans[k]].astype(F32)).astype(BF16)
        s1n.append([
            copy(qsum.at[next_f, every, spans[k]], s1b.at[0, every, spans[k]], sem_rs, 6 + 2 * k, first_peer(1)),
            copy(qsum.at[last_f, every, spans[k]], s1b.at[1, every, spans[k]], sem_rs, 7 + 2 * k, first_peer(3)),
        ])
        for c in s1n[k]:
            c.start()

    w3[2].wait_recv()
    w4.append(wcopy(last_f, every, 25, sibling))
    w4[1].start()
    w3[3].wait_recv()
    w4.append(wcopy(next_f, every, 26, sibling))
    w4[2].start()
    for c in w5:
        c.wait_recv()
    w4.append(wcopy(far_f, every, 27, sibling))
    w4[3].start()

    def tap_weight(h, p, kind):
        lanes = []
        for ll in range(2):
            parts = []
            for dd in range(8):
                f, s = piece(h, dd, ll)
                parts.append(wall[h, f, s, strip(p, kind), :])
            lanes.append(jnp.concatenate(parts, axis=0))
        return jnp.concatenate(lanes, axis=1)

    def tap_weights(h, p):
        shared = tap_weight(h, p, 2)
        return [jnp.concatenate([tap_weight(h, p, kind), shared], axis=0) for kind in range(2)]

    def grad_tap(tap, tail):
        a, be = tap_of(tap)
        rows_ = pl.ds(pl.multiple_of((2 - a) * 64, 64), 256)
        return jnp.concatenate([gsh[8 - be, rows_, 0:128], gsh[8 - be, rows_, 128 * tail : 128 * tail + 128]], axis=1)

    def hidden_half(h, fresh):
        for p in range(7):
            tap = h * 14 + 2 * p
            wa, wb = tap_weights(h, p)
            lhs = jnp.concatenate([grad_tap(tap, 1), grad_tap(tap + 1, 2)], axis=1)
            value = dot(lhs, jnp.concatenate([wa, wb], axis=0))
            if fresh and p == 0:
                acc_h[...] = value
            else:
                acc_h[...] += value

    def conv_half(h, fresh):
        for group in ((0, 1), (2, 3), (4, 5), (6,)):
            both = [tap_weights(h, p) for p in group]
            for odd, acc in enumerate((acc_e, acc_o)):
                lhs = jnp.concatenate([hidden_tap(h * 14 + 2 * p + odd) for p in group], axis=1)
                rhs = jnp.concatenate([w[odd] for w in both], axis=1)
                value = lax.dot_general(lhs, rhs, NT_DIMS, preferred_element_type=F32)
                if fresh and group[0] == 0:
                    acc[...] = value
                else:
                    acc[...] += value

    hidden_half(core, True)

    for pair in s1n:
        for c in pair:
            c.wait_recv()

    def first_total(s):
        return qsum[own_f, s].astype(F32) + s1b[0, s].astype(F32) + s1b[1, s].astype(F32)

    def add_first(s, carry):
        rsum[s] = first_total(s).astype(BF16)
        return carry

    lax.fori_loop(0, 4, add_first, 0)
    s2 = [copy(rsum.at[(own_s + j) % 4], s2buf.at[j - 1], sem_rs, 9 + j, second_peer(j)) for j in (1, 2, 3)]
    for c in s2:
        c.start()
    for c in w4:
        c.wait_recv()
    hidden_half(other, False)

    dn = acc_h[...] * dfac_s[...]
    back = pack_stats(jnp.sum(dn, axis=0, keepdims=True), jnp.sum(dn * normed_s[...], axis=0, keepdims=True))
    acc_h[...] = dn
    all_bk[t] = back
    bk = to_all(all_bk, sem_bk)

    for c in s2:
        c.wait_recv()
    total = first_total(own_s)
    for j in range(3):
        total = total + s2buf[j].astype(F32)
    total = jnp.concatenate([total, jnp.zeros((48, 128), F32)], axis=0).T.reshape(8, 2, 8, 384)
    s3own[...] = total
    s3src[...] = total.astype(BF16)
    s3 = [copy(s3src.at[(z + j) % 8, core], s3buf.at[core, j], sem_rs, 12 + j, z_peer(j)) for j in range(1, 8)]
    s3 += [copy(s3src.at[(z + j) % 8, other], s3buf.at[core, j], sem_rs, 20 + j, device(x, y, (z + j) % 8, other)) for j in range(8)]
    for c in s3:
        c.start()

    conv_half(core, True)
    conv_half(other, False)

    lane256 = iota((256, 192), 0)
    pack_out = one_hot(jnp.where(lane256 < 128, out_channel(lane256), jnp.where((lane256 & 15) < 8, out_channel(lane256), -1)) == iota((256, 192), 1), BF16)
    bias_l = exact_dot(bias[...], spread_out[:, 0:256].astype(F32))
    tail_odd = pltpu.roll(acc_o[:, 128:256], 120, 1)
    conv = jnp.concatenate([acc_e[:, 0:128] + acc_o[:, 0:128], acc_e[:, 128:256] + tail_odd], axis=1)
    conv = ((conv + bias_l) * vmask2).astype(BF16)
    conv_out[...] = dot(conv, pack_out).astype(BF16)

    sum_one, sum_two = clip_sums(all_bk, bk)
    pack_in = one_hot(in_channel(iota((256, 192), 0)) == iota((256, 192), 1), BF16)
    grad_x = inv_std * (acc_h[...] - sum_one - normed_s[...] * sum_two) * vmask2
    in_grad[...] = dot(grad_x.astype(BF16), pack_in).astype(BF16)

    for c in s3:
        c.wait_recv()
    own_rows, other_rows = s3own[z, core], s3buf[other, 0].astype(F32)
    for j in range(1, 8):
        own_rows = own_rows + s3buf[core, j].astype(F32)
        other_rows = other_rows + s3buf[other, j].astype(F32)

    def unpack(value, h):
        flat = (value[0:6].reshape(6, 1, 384) * out_mask[None]).reshape(144, 384)
        high = flat.astype(BF16)
        low = (flat - high.astype(F32)).astype(BF16)
        return sum(lax.dot_general(v, sel_s[h], NT_DIMS, preferred_element_type=F32) for v in (high, low))

    wg_out[...] = (unpack(own_rows, core) + unpack(other_rows, other)).reshape(6, 24, 27)
    for c in zw + w2 + w3 + w4 + w5 + s0 + s1[0] + s1[1] + s1n[0] + s1n[1] + s2 + s3 + st + bk + halos:
        c.wait_send()


def emit(conv, grad, wg, conv_out, grad_out, wg_out):
    conv_out[...] = conv[...]
    grad_out[...] = grad[...]
    wg_out[...] = wg[...]


def on_device(features, out_grad, weight, bias, gamma, beta, tile_clip, tile_rows, clip_cols, clip_start):
    dma = pltpu.SemaphoreType.DMA
    vmem, anywhere = pl.BlockSpec(memory_space=pltpu.VMEM), pl.BlockSpec(memory_space=pl.ANY)
    conv_out, in_grad, wg = pl.pallas_call(
        kernel,
        out_shape=(
            jax.ShapeDtypeStruct((256, 192), BF16),
            jax.ShapeDtypeStruct((256, 192), BF16),
            jax.ShapeDtypeStruct((6, 24, 27), F32),
        ),
        in_specs=[anywhere] * 12,
        out_specs=[vmem] * 3,
        scratch_shapes=[
            pltpu.VMEM((2, 4, 8, 192), BF16),
            pltpu.VMEM((2, 4, 8, 192), BF16),
            pltpu.VMEM((32, 4, 128), F32),
            pltpu.VMEM((32, 4, 128), F32),
            pltpu.VMEM((2, 8, 384), BF16),
            pltpu.VMEM((2, 27, 384), BF16),
            pltpu.VMEM((8, 2, 8, 384), BF16),
            pltpu.VMEM((2, 4, 4, 336, 128), BF16),
            pltpu.VMEM((9, 384, 256), BF16),
            pltpu.VMEM((9, 384, 384), BF16),
            pltpu.VMEM((512, 256), BF16),
            pltpu.VMEM((4, 4, 336, 128), BF16),
            pltpu.VMEM((4, 4, 336, 128), BF16),
            pltpu.VMEM((4, 4, 336, 128), BF16),
            pltpu.VMEM((2, 2, 336, 128), BF16),
            pltpu.VMEM((2, 4, 336, 128), BF16),
            pltpu.VMEM((4, 336, 128), BF16),
            pltpu.VMEM((3, 336, 128), BF16),
            pltpu.VMEM((8, 2, 8, 384), F32),
            pltpu.VMEM((8, 2, 8, 384), BF16),
            pltpu.VMEM((2, 8, 8, 384), BF16),
            pltpu.VMEM((256, 256), F32),
            pltpu.VMEM((256, 256), F32),
            pltpu.VMEM((256, 256), F32),
            pltpu.VMEM((256, 256), F32),
            pltpu.VMEM((256, 256), F32),
            pltpu.SMEM((1, 32), I32),
            pltpu.SMEM((1, 32), I32),
            pltpu.SMEM((1, 32), I32),
            pltpu.SMEM((1, 32), I32),
            pltpu.VMEM((256, 192), BF16),
            pltpu.VMEM((256, 192), BF16),
            pltpu.VMEM((6, 24, 27), BF16),
            pltpu.VMEM((1, 192), F32),
            pltpu.VMEM((1, 192), F32),
            pltpu.VMEM((1, 192), F32),
            dma((10,)),
            dma((2, 4)),
            dma((2, 31)),
            dma((2, 31)),
            dma((2, 28)),
            dma((2, 28)),
        ],
        compiler_params=pltpu.CompilerParams(collective_id=0, has_side_effects=True, vmem_limit_bytes=56 * 1024 * 1024),
    )(
        tile_clip, tile_rows, clip_cols, clip_start,
        features.reshape(256, 192), features.reshape(4, 8, 8, 192),
        out_grad.reshape(256, 192), out_grad.reshape(4, 8, 8, 192),
        weight.transpose(0, 2, 1), gamma.reshape(1, 192), beta.reshape(1, 192), bias.reshape(1, 192),
    )
    conv_out, in_grad, wg = pl.pallas_call(
        emit,
        out_shape=tuple(jax.ShapeDtypeStruct(v.shape, v.dtype) for v in (conv_out, in_grad, wg)),
        in_specs=[vmem] * 3,
        out_specs=[vmem] * 3,
    )(conv_out, in_grad, wg)
    return (conv_out.reshape(features.shape), in_grad.reshape(features.shape), wg.transpose(0, 2, 1))


def solution(mesh):
    in_specs = (
        P("dp", None, "tile", None, None),
        P("dp", None, "tile", None, None),
        P("tile", None, "dp"),
        P(),
        P(),
        P(),
        P("dp", None),
        P("dp", None),
        P("dp", None),
        P("dp", None),
    )
    out_specs = (
        P("dp", None, "tile", None, None),
        P("dp", None, "tile", None, None),
        P("tile", None, "dp"),
    )
    return jax.shard_map(on_device, mesh=mesh, in_specs=in_specs, out_specs=out_specs, check_vma=False)
```
